128 devices in a mesh: col: 8 (over x, y_lo), sec: 16 (over y_hi, z, core).
Axes of the slice: x: 4, y: 4 (y_hi: 2, y_lo: 2; y = y_hi * 2 + y_lo), z: 4, core: 2. Of those that a mesh axis runs over, the one named last changes fastest.
Arguments:
- thermal_state: float32 [128, 128, 256], P('sec', 'col'), may hold values from -6 to 6
- flow_vector: float32 [2, 128, 128, 256], P(None, 'sec', 'col'), may hold values from -5 to 5
- vertical_spreading: float32 [128, 128, 256], P('sec', 'col'), may hold values from 0.05 to 0.5
- solute_fields: float32 [32, 128, 128, 256], P('sec', None, 'col'), may hold values from 0.1 to 2
- linear_exchange_speeds: float32 [32, 32], replicated, may hold values from -1 to 1
- newton_preconditioner: float32 [32, 32], replicated, may hold values from -0.6 to 1.2
- absorption_speed: float32 [32], replicated, may hold values from 0.2 to 2
- water_indicator: int32 [128, 256], P('col'), may hold values from 0 to 1, as said below
Outputs:
- thermal_revised: float32 [128, 128, 256], P('sec', 'col')
- velocity_next: float32 [2, 128, 128, 256], P(None, 'sec', 'col')
- diffusivity_next: float32 [128, 128, 256], P('sec', 'col')
- solute_revised: float32 [32, 128, 128, 256], P('sec', None, 'col')
The draws below stay inside these ranges and needn't reach their ends.
Inputs may be any that keep to these rules, and one draw needn't show every extreme that they name: `water_indicator`: in each block of 16 consecutive longitudes, between 1536 and 3072 columns are wet, and some block holds exactly 3072 wet columns.
All inputs are finite; a program needn't handle non-finite values.
Results may differ from the reference program's by a relative error of at most 0.0001.
Values sent between devices are 32-bit elements; how exact they have to be, the bound alone decides.
A program may use at most 128 MiB of HBM per device.

```python
import math
import jax
import jax.numpy as jnp
from jax import lax

XD = 16
PARALLEL_TOTAL = 256
LAYER_TOTAL = 128
NTR = 32
NEWTON = 2
MERIDIAN_TOTAL = 128


def draw_newton_preconditioner(key, part):
    spread = 0.25 * jax.random.normal(jax.random.fold_in(key, 11), (NTR, NTR), jnp.float32)
    spread = jnp.clip(spread / jnp.sqrt(NTR * 1.0), -0.55, 0.55)
    return (0.6 * jnp.eye(NTR, dtype=jnp.float32) + spread).astype(jnp.float32)


def draw_water_indicator(key, part):
    blocks = MERIDIAN_TOTAL // XD
    columns = XD * PARALLEL_TOTAL
    most = 3 * columns // 4
    counts = jax.random.randint(jax.random.fold_in(key, 21), (blocks,), most // 2, most + 1)
    fullest = jax.random.randint(jax.random.fold_in(key, 22), (), 0, blocks)
    counts = jnp.where(jnp.arange(blocks) == fullest, most, counts)
    ranks = jax.vmap(lambda sub: jax.random.permutation(sub, columns))(jax.random.split(jax.random.fold_in(key, 23), blocks))
    return (ranks < counts[:, None]).astype(jnp.int32).reshape(MERIDIAN_TOTAL, PARALLEL_TOTAL)


def levels(stream_key, dims, pieces, low, top_value):
    def one(axis_at, blocks):
        draws = jax.random.uniform(jax.random.fold_in(jax.random.fold_in(stream_key, 6), axis_at), (blocks,), jnp.float32, low / len(pieces), top_value / len(pieces))
        return jnp.repeat(jnp.exp(draws), dims[axis_at] // blocks).reshape((-1,) + (1,) * (len(dims) - axis_at - 1))

    level = one(*pieces[0])
    for cut in pieces[1:]:
        level = level * one(*cut)
    return level


def noise(stream_key, shape, scale, reach, shards=(), kind=jnp.bfloat16):
    entries = jax.random.normal(stream_key, shape, jnp.float32) * scale
    if len(shards) > 0:
        entries = levels(stream_key, shape, shards, -0.22, 0.18) * entries
    return jnp.clip(entries, min=-reach, max=reach).astype(kind)


def setup_inputs(seed: int = 0) -> dict:
    splits = jax.random.split(jax.random.key(seed), 9)
    thermal_state = noise(splits[0], (LAYER_TOTAL, MERIDIAN_TOTAL, PARALLEL_TOTAL), 1.0, 6.0, ((0, 16), (1, 8)), jnp.float32)
    flow_vector = noise(splits[1], (2, LAYER_TOTAL, MERIDIAN_TOTAL, PARALLEL_TOTAL), 1.0, 5.0, ((1, 16), (2, 8)), jnp.float32)
    vertical_spreading = jnp.clip(jnp.exp(math.log(0.5) - 2.3025851 * jax.random.uniform(splits[2], (LAYER_TOTAL, MERIDIAN_TOTAL, PARALLEL_TOTAL), jnp.float32) ** levels(splits[2], (LAYER_TOTAL, MERIDIAN_TOTAL, PARALLEL_TOTAL), ((0, 16), (1, 8)), -0.2, 0.2)), 0.05, 0.5)
    solute_fields = jnp.clip(jnp.exp(math.log(2.0) - 2.9957323 * jax.random.uniform(splits[3], (NTR, LAYER_TOTAL, MERIDIAN_TOTAL, PARALLEL_TOTAL), jnp.float32) ** levels(splits[3], (NTR, LAYER_TOTAL, MERIDIAN_TOTAL, PARALLEL_TOTAL), ((0, 16), (2, 8)), -0.2, 0.2)), 0.1, 2.0)
    linear_exchange_speeds = noise(splits[4], (NTR, NTR), NTR ** -0.5, 1.0, (), jnp.float32)
    newton_preconditioner = draw_newton_preconditioner(jax.random.fold_in(splits[8], 71), 0)
    absorption_speed = jnp.clip(jnp.exp(jax.random.uniform(splits[6], (NTR,), jnp.float32, math.log(0.2), math.log(2.0))), 0.2, 2.0)
    water_indicator = draw_water_indicator(jax.random.fold_in(splits[8], 71), 0)
    return dict(thermal_state=thermal_state, flow_vector=flow_vector, vertical_spreading=vertical_spreading, solute_fields=solute_fields, linear_exchange_speeds=linear_exchange_speeds, newton_preconditioner=newton_preconditioner, absorption_speed=absorption_speed, water_indicator=water_indicator)


CORIOLIS = 0.8
MIXING = 0.1
ADVECTION = 0.2
VERTICAL_MIX = 0.3
WATER_ABSORB = 0.02
PIGMENT_ABSORB = 0.06
CHLOROPHYLL_WARM = 10.0


def latitude_terms(count):
    index = jnp.arange(count).astype(jnp.float32)
    latitude = jnp.pi * (index + 0.5) / count - jnp.pi / 2
    return jnp.sin(latitude), jnp.cos(latitude)


def chemical_change(center, eastern, western, east_flow, north_flow):
    northern = jnp.concatenate([center[..., 1:], center[..., -1:]], axis=-1)
    southern = jnp.concatenate([center[..., :1], center[..., :-1]], axis=-1)
    laplace = eastern + western + northern + southern - 4.0 * center
    return MIXING * laplace - 0.5 * ADVECTION * (east_flow * (eastern - western) + north_flow * (northern - southern))


def column_mixing(field, kappa):
    weights = VERTICAL_MIX * kappa[:-1]
    fluxes = weights[None] * (field[:, 1:] - field[:, :-1])
    zeros = jnp.zeros_like(fluxes[:, :1])
    return jnp.concatenate([fluxes, zeros], axis=1) - jnp.concatenate([zeros, fluxes], axis=1)


def react(start, linear_exchange_speeds, newton_preconditioner, absorption_speed):
    rates = absorption_speed.reshape((-1,) + (1,) * (start.ndim - 1))
    current = start
    for step in range(NEWTON):
        linear = jnp.einsum("ij,j...->i...", linear_exchange_speeds, current, precision=lax.Precision.HIGHEST)
        square = current * current
        rate = linear - rates * square / (1.0 + square)
        misfit = current - start - rate
        current = current - jnp.einsum("ij,j...->i...", newton_preconditioner, misfit, precision=lax.Precision.HIGHEST)
    return current


def heating(pigment_tracer, shortwave):
    square = pigment_tracer * pigment_tracer
    absorb = WATER_ABSORB + PIGMENT_ABSORB * square / (1.0 + square)
    depth = jnp.cumsum(absorb, axis=0)
    return shortwave * (jnp.exp(-(depth - absorb)) - jnp.exp(-depth))


def reference(thermal_state, flow_vector, vertical_spreading, solute_fields, linear_exchange_speeds, newton_preconditioner, absorption_speed, water_indicator):
    sines, cosines = latitude_terms(PARALLEL_TOTAL)
    rotation = CORIOLIS * sines
    divisor = 1.0 + rotation * rotation
    zonal_flow_speed = (flow_vector[0] + rotation * flow_vector[1]) / divisor
    meridional_flow_speed = (flow_vector[1] - rotation * flow_vector[0]) / divisor
    zero_level = jnp.zeros_like(zonal_flow_speed[:1])
    east_below = jnp.concatenate([zonal_flow_speed[1:], zero_level], axis=0)
    north_below = jnp.concatenate([meridional_flow_speed[1:], zero_level], axis=0)
    shear = (zonal_flow_speed - east_below) ** 2 + (meridional_flow_speed - north_below) ** 2
    spreading_revised = 0.5 * vertical_spreading + 0.5 * shear / (1.0 + shear)
    thermal_carried = thermal_state + chemical_change(thermal_state, jnp.roll(thermal_state, -1, axis=1), jnp.roll(thermal_state, 1, axis=1), zonal_flow_speed, meridional_flow_speed)
    water_sites = water_indicator.astype(jnp.float32)
    moved = solute_fields + water_sites * (chemical_change(solute_fields, jnp.roll(solute_fields, -1, axis=2), jnp.roll(solute_fields, 1, axis=2), zonal_flow_speed, meridional_flow_speed) + column_mixing(solute_fields, spreading_revised))
    reacted = react(moved, linear_exchange_speeds, newton_preconditioner, absorption_speed)
    solute_revised = jnp.where(water_indicator > 0, reacted, moved)
    warming_quantity = heating(solute_revised[0], cosines)
    thermal_revised = thermal_carried + CHLOROPHYLL_WARM * water_sites * warming_quantity
    return thermal_revised, jnp.stack([zonal_flow_speed, meridional_flow_speed]), spreading_revised, solute_revised
```

```python
import jax
import jax.numpy as jnp
import numpy as np
from jax import lax
from jax.experimental import pallas as pl
from jax.experimental.pallas import tpu as pltpu
from jax.sharding import PartitionSpec as P

CORIOLIS = 0.8
MIXING = 0.1
VERTICAL_MIX = 0.3
WATER_ABSORB = 0.02
PIGMENT_ABSORB = 0.06
CHLOROPHYLL_WARM = 10.0

SECS = 16
COLS = 8
LEV = 8
LON = 16
TR = 32
LAT = 256
MESH = pl.DeviceIdType.MESH
F32 = jnp.float32
BF16 = jnp.bfloat16
HIGHEST = lax.Precision.HIGHEST


def saturating(value):
    return 1.0 - 1.0 / (1.0 + value * value)


def stacked_halves(top, bottom):
    both = jnp.concatenate([top, bottom], axis=0)
    high = both.astype(BF16)
    low = (both - high.astype(F32)).astype(BF16)
    return jnp.concatenate([high, low, high, low], axis=0)


def kernel(
    x, flow, kap, th, lin, pre, ab, wat, lat,
    th_o, vel_o, kap_o, sol_o,
    R, S, coef, lhs, flow_v, kap_v, th_v, lin_v, pre_v, ab_v, wat_v, lat_v,
    below_v, above_v, kabove_v, thh, vel_v, knext_v, pig, totals, thn_v,
    lsem, osem, small_s, small_r, hs, hr, fs, fr, vs, vr, bs, br, ps, ts, tr_,
):
    c = lax.axis_index("col")
    s = lax.axis_index("sec")
    left, right = (c + COLS - 1) % COLS, (c + 1) % COLS
    up, down = (s + SECS - 1) % SECS, (s + 1) % SECS

    loads = [
        pltpu.make_async_copy(a, b, lsem.at[i])
        for i, (a, b) in enumerate(
            [(flow, flow_v), (kap, kap_v), (th, th_v), (lin, lin_v), (pre, pre_v), (ab, ab_v), (wat, wat_v), (lat, lat_v)]
        )
    ]
    for copy in loads:
        copy.start()

    barrier = pltpu.get_barrier_semaphore()

    def greet(r, _):
        @pl.when(r > 0)
        def _():
            pl.semaphore_signal(barrier, inc=1, device_id=(c, s ^ r), device_id_type=MESH)

        pl.semaphore_signal(barrier, inc=1, device_id=(left, s ^ r), device_id_type=MESH)
        pl.semaphore_signal(barrier, inc=1, device_id=(right, s ^ r), device_id_type=MESH)
        return 0

    lax.fori_loop(0, SECS, greet, 0)
    pl.semaphore_wait(barrier, 3 * SECS - 1)

    def remote(src, dst, send, recv, to):
        return pltpu.make_async_remote_copy(
            src_ref=src, dst_ref=dst, send_sem=send, recv_sem=recv, device_id=to, device_id_type=MESH
        )

    smalls = [
        remote(flow.at[:, 0], below_v, small_s.at[0], small_r.at[0], (c, up)),
        remote(flow.at[:, LEV - 1], above_v, small_s.at[1], small_r.at[1], (c, down)),
        remote(kap.at[LEV - 1], kabove_v, small_s.at[2], small_r.at[2], (c, down)),
        remote(th.at[:, 0, :], thh.at[1, :, 0, :], small_s.at[3], small_r.at[3], (left, s)),
        remote(th.at[:, LON - 1, :], thh.at[0, :, 0, :], small_s.at[4], small_r.at[4], (right, s)),
    ]
    for copy in smalls:
        copy.start()

    def edges(r, _):
        d = s ^ r
        for t in range(2):
            remote(
                x.at[t, pl.ds(LEV * d, LEV), 0, :], R.at[pl.ds(1, LEV), LON + 1, 2 * s + t, :],
                hs, hr, (left, d),
            ).start()
            remote(
                x.at[t, pl.ds(LEV * d, LEV), LON - 1, :], R.at[pl.ds(1, LEV), 0, 2 * s + t, :],
                hs, hr, (right, d),
            ).start()
        return 0

    lax.fori_loop(0, SECS, edges, 0)

    def forward(i, _):
        k = lax.select(i == 1, LEV - 1, lax.select(i == 0, 0, i - 1))
        for t in range(2):
            pltpu.make_async_copy(
                x.at[t, LEV * s + k], R.at[k + 1, pl.ds(1, LON), 2 * s + t, :], fr.at[k]
            ).start()

        def peer(r, _):
            d = s ^ r
            for t in range(2):
                remote(
                    x.at[t, LEV * d + k], R.at[k + 1, pl.ds(1, LON), 2 * s + t, :],
                    fs.at[k], fr.at[k], (c, d),
                ).start()
            return 0

        lax.fori_loop(1, SECS, peer, 0)
        return 0

    lax.fori_loop(0, LEV, forward, 0)

    for copy in loads:
        copy.wait()
    for copy in smalls:
        copy.wait()

    rot = jnp.broadcast_to(lat_v[0:1, :], (LON, LAT))
    inv = 1.0 + rot * rot
    wet = wat_v[...].astype(F32)
    row = lax.broadcasted_iota(jnp.int32, (LON, LAT), 0)
    lane = lax.broadcasted_iota(jnp.int32, (LON, LAT), 1)

    def turned(u, v):
        return (u + rot * v) / inv, (v - rot * u) / inv

    below_ok = jnp.where(s == SECS - 1, 0.0, 1.0)
    above_ok = jnp.where(s == 0, 0.0, 1.0)
    east_a, north_a = turned(above_v[0], above_v[1])
    east_b, north_b = turned(below_v[0], below_v[1])
    east, north = turned(flow_v[0, 0], flow_v[1, 0])
    shear = (east_a - east) ** 2 + (north_a - north) ** 2
    k_up = (0.5 * kabove_v[...] + 0.5 * shear / (1.0 + shear)) * (VERTICAL_MIX * above_ok) * wet
    for k in range(LEV):
        vel_v[0, k] = east
        vel_v[1, k] = north
        if k < LEV - 1:
            east_n, north_n = turned(flow_v[0, k + 1], flow_v[1, k + 1])
        else:
            east_n, north_n = east_b * below_ok, north_b * below_ok
        shear = (east - east_n) ** 2 + (north - north_n) ** 2
        knext = 0.5 * kap_v[k] + 0.5 * shear / (1.0 + shear)
        knext_v[k] = knext
        k_down = knext * VERTICAL_MIX * wet
        if k == LEV - 1:
            k_down = k_down * below_ok
        coef[k, 0] = (1.0 - 4.0 * MIXING * wet) - k_down - k_up
        coef[k, 1] = (MIXING - MIXING * east) * wet
        coef[k, 2] = (MIXING + MIXING * east) * wet
        coef[k, 3] = (MIXING - MIXING * north) * wet
        coef[k, 4] = (MIXING + MIXING * north) * wet
        coef[k, 5] = k_down
        coef[k, 6] = k_up
        f = th_v[k]
        f_e = jnp.where(row == LON - 1, jnp.broadcast_to(thh[1, k, 0:1, :], (LON, LAT)), pltpu.roll(f, LON - 1, 0))
        f_w = jnp.where(row == 0, jnp.broadcast_to(thh[0, k, 0:1, :], (LON, LAT)), pltpu.roll(f, 1, 0))
        f_n = jnp.where(lane == LAT - 1, f, pltpu.roll(f, LAT - 1, 1))
        f_s = jnp.where(lane == 0, f, pltpu.roll(f, 1, 1))
        thn_v[k] = (
            f + MIXING * (f_e + f_w + f_n + f_s - 4.0 * f)
            - MIXING * (east * (f_e - f_w) + north * (f_n - f_s))
        )
        east, north, k_up = east_n, north_n, k_down
    outs = [pltpu.make_async_copy(vel_v, vel_o, osem.at[0]), pltpu.make_async_copy(knext_v, kap_o, osem.at[1])]
    for copy in outs:
        copy.start()

    inner = jnp.dot(pre_v[...], lin_v[...], precision=HIGHEST, preferred_element_type=F32)
    scaled = pre_v[...] * ab_v[...]
    at = lax.broadcasted_iota(jnp.int32, (TR, LAT), 1)
    which = lax.broadcasted_iota(jnp.int32, (TR, LAT), 0)
    pick_m = (at % (2 * TR) == which).astype(F32)
    pick_s = (at % (2 * TR) == which + TR).astype(F32)
    first = jnp.dot(inner, pick_m, precision=HIGHEST, preferred_element_type=F32) - jnp.dot(
        scaled, pick_s, precision=HIGHEST, preferred_element_type=F32
    )
    second = -jnp.dot(pre_v[...], first, precision=HIGHEST, preferred_element_type=F32)
    for i, rows in enumerate((first, second)):
        high = rows.astype(BF16)
        low = rows - high.astype(F32)
        lhs[pl.ds(TR * i, TR), :] = jnp.where(at < 4 * TR, high.astype(F32), low).astype(BF16)

    def all_of(k, sem):
        pltpu.make_async_copy(R.at[k + 1, pl.ds(1, LON)], R.at[k + 1, pl.ds(1, LON)], sem).wait()

    all_of(0, fr.at[0])
    all_of(LEV - 1, fr.at[LEV - 1])
    verticals = [
        remote(R.at[1, pl.ds(1, LON)], R.at[LEV + 1, pl.ds(1, LON)], vs.at[0], vr.at[0], (c, up)),
        remote(R.at[LEV, pl.ds(1, LON)], R.at[0, pl.ds(1, LON)], vs.at[1], vr.at[1], (c, down)),
    ]
    for copy in verticals:
        copy.start()
    edge = R.at[pl.ds(1, LEV), pl.ds(0, 2)]
    pltpu.make_async_copy(edge, edge, hr).wait()
    all_of(1, fr.at[1])

    tlane = lax.broadcasted_iota(jnp.int32, (TR, LAT), 1)

    def level(i, _):
        k = lax.select(i == LEV - 1, LEV - 1, lax.select(i == LEV - 2, 0, i + 1))

        @pl.when(i < LEV - 3)
        def _():
            all_of(i + 2, fr.at[i + 2])

        @pl.when(i == LEV - 2)
        def _():
            verticals[1].wait_recv()

        @pl.when(i == LEV - 1)
        def _():
            verticals[0].wait_recv()

        def column(j, _):
            def row_of(n):
                return jnp.broadcast_to(coef[k, n, pl.ds(j, 1), :], (TR, LAT))

            center = R[k + 1, j + 1]
            moved = row_of(0) * center
            moved += row_of(1) * R[k + 1, j + 2]
            moved += row_of(2) * R[k + 1, j]
            moved += row_of(3) * jnp.where(tlane == LAT - 1, center, pltpu.roll(center, LAT - 1, 1))
            moved += row_of(4) * jnp.where(tlane == 0, center, pltpu.roll(center, 1, 1))
            moved += row_of(5) * R[k + 2, j + 1]
            moved += row_of(6) * R[k, j + 1]
            y = jnp.dot(lhs[...], stacked_halves(moved, saturating(moved)), preferred_element_type=F32)
            current = moved + y[:TR]
            base = current + y[TR:]
            y = jnp.dot(lhs[:TR, :], stacked_halves(current, saturating(current)), preferred_element_type=F32)
            wet_row = jnp.broadcast_to(wat_v[pl.ds(j, 1), :], (TR, LAT))
            S[k, j] = jnp.where(wet_row > 0, base + y, moved)
            return 0

        lax.fori_loop(0, LON, column, 0, unroll=2)

        pltpu.make_async_copy(S.at[k, :, 0, :], pig.at[k], ps).start()
        for t in range(2):
            pltpu.make_async_copy(S.at[k, :, 2 * s + t, :], sol_o.at[t, LEV * s + k], br.at[k]).start()

        def peer(r, _):
            d = s ^ r
            for t in range(2):
                remote(
                    S.at[k, :, 2 * d + t, :], sol_o.at[t, LEV * s + k], bs.at[k], br.at[k], (c, d)
                ).start()
            return 0

        lax.fori_loop(1, SECS, peer, 0)
        return 0

    lax.fori_loop(0, LEV, level, 0)

    pltpu.make_async_copy(pig, pig, ps).wait()
    total = jnp.zeros((LON, LAT), F32)
    for k in range(LEV):
        total += WATER_ABSORB + PIGMENT_ABSORB * saturating(pig[k])
    totals[s] = total

    def tell(r, _):
        remote(totals.at[s], totals.at[s], ts, tr_, (c, s ^ r)).start()
        return 0

    lax.fori_loop(1, SECS, tell, 0)
    others = totals.at[pl.ds(0, SECS - 1)]
    pltpu.make_async_copy(others, others, tr_).wait()
    depth = jnp.zeros((LON, LAT), F32)
    for d in range(SECS):
        depth += totals[d] * jnp.where(d < s, 1.0, 0.0)
    light = CHLOROPHYLL_WARM * jnp.broadcast_to(lat_v[1:2, :], (LON, LAT)) * wet
    before = jnp.exp(-depth)
    for k in range(LEV):
        depth = depth + (WATER_ABSORB + PIGMENT_ABSORB * saturating(pig[k]))
        after = jnp.exp(-depth)
        thn_v[k] = thn_v[k] + light * (before - after)
        before = after
    outs.append(pltpu.make_async_copy(thn_v, th_o, osem.at[2]))
    outs[-1].start()

    pltpu.make_async_copy(others, others, ts).wait()
    pltpu.make_async_copy(edge, edge, hs).wait()
    for copy in verticals:
        copy.wait_send()
    sent = R.at[1, pl.ds(1, LON - 1)]

    def finish(k, _):
        pltpu.make_async_copy(sent, sent, fs.at[k]).wait()
        pltpu.make_async_copy(sent, sent, bs.at[k]).wait()
        back = sol_o.at[0, pl.ds(0, 2 * SECS)]
        pltpu.make_async_copy(back, back, br.at[k]).wait()
        return 0

    lax.fori_loop(0, LEV, finish, 0)
    for copy in outs:
        copy.wait()


def on_device(thermal, flow, spreading, solute, lin, pre, ab, water):
    index = (np.arange(LAT, dtype=np.float64) + 0.5) * np.pi / LAT - np.pi / 2
    table = np.zeros((8, LAT), np.float32)
    table[0] = CORIOLIS * np.sin(index)
    table[1] = np.cos(index)
    hbm = pl.BlockSpec(memory_space=pl.ANY)
    dma = pltpu.SemaphoreType.DMA
    return pl.pallas_call(
        kernel,
        out_shape=(
            jax.ShapeDtypeStruct(thermal.shape, F32),
            jax.ShapeDtypeStruct(flow.shape, F32),
            jax.ShapeDtypeStruct(spreading.shape, F32),
            jax.ShapeDtypeStruct(solute.shape, F32),
        ),
        in_specs=[hbm] * 9,
        out_specs=(hbm,) * 4,
        scratch_shapes=[
            pltpu.VMEM((LEV + 2, LON + 2, TR, LAT), F32),
            pltpu.VMEM((LEV, LON, TR, LAT), F32),
            pltpu.VMEM((LEV, 7, LON, LAT), F32),
            pltpu.VMEM((2 * TR, LAT), BF16),
            pltpu.VMEM((2, LEV, LON, LAT), F32),
            pltpu.VMEM((LEV, LON, LAT), F32),
            pltpu.VMEM((LEV, LON, LAT), F32),
            pltpu.VMEM((TR, TR), F32),
            pltpu.VMEM((TR, TR), F32),
            pltpu.VMEM((1, TR), F32),
            pltpu.VMEM((LON, LAT), jnp.int32),
            pltpu.VMEM((8, LAT), F32),
            pltpu.VMEM((2, LON, LAT), F32),
            pltpu.VMEM((2, LON, LAT), F32),
            pltpu.VMEM((LON, LAT), F32),
            pltpu.VMEM((2, LEV, 8, LAT), F32),
            pltpu.VMEM((2, LEV, LON, LAT), F32),
            pltpu.VMEM((LEV, LON, LAT), F32),
            pltpu.VMEM((LEV, LON, LAT), F32),
            pltpu.VMEM((SECS, LON, LAT), F32),
            pltpu.VMEM((LEV, LON, LAT), F32),
            dma((8,)), dma((3,)), dma((5,)), dma((5,)),
            dma, dma, dma((LEV,)), dma((LEV,)), dma((2,)), dma((2,)), dma((LEV,)), dma((LEV,)),
            dma, dma, dma,
        ],
        compiler_params=pltpu.CompilerParams(
            collective_id=0, has_side_effects=True, vmem_limit_bytes=56 << 20
        ),
        name="ocean_step",
    )(solute, flow, spreading, thermal, lin, pre, ab.reshape(1, TR), water, jnp.asarray(table))


def solution(mesh):
    placed = (
        P("sec", "col", None),
        P(None, "sec", "col", None),
        P("sec", "col", None),
        P("sec", None, "col", None),
        P(),
        P(),
        P(),
        P("col", None),
    )
    return jax.shard_map(
        on_device,
        mesh=mesh,
        in_specs=placed,
        out_specs=placed[:1] + placed[1:4],
        check_vma=False,
    )
```

```python
import jax
import jax.numpy as jnp
import numpy as np
from jax import lax
from jax.experimental import pallas as pl
from jax.experimental.pallas import tpu as pltpu
from jax.sharding import PartitionSpec as P

CORIOLIS = 0.8
MIXING = 0.1
VERTICAL_MIX = 0.3
WATER_ABSORB = 0.02
PIGMENT_ABSORB = 0.06
CHLOROPHYLL_WARM = 10.0

SECS = 16
COLS = 8
LEV = 8
LON = 16
TR = 32
LAT = 256
AHEAD = 4
MESH = pl.DeviceIdType.MESH
F32 = jnp.float32
BF16 = jnp.bfloat16
HIGHEST = lax.Precision.HIGHEST


def saturating(value):
    return 1.0 - 1.0 / (1.0 + value * value)


def stacked_halves(top, bottom):
    both = jnp.concatenate([top, bottom], axis=0)
    high = both.astype(BF16)
    low = (both - high.astype(F32)).astype(BF16)
    return jnp.concatenate([high, low, high, low], axis=0)


def kernel(
    x, flow, kap, th, lin, pre, ab, wat, lat,
    th_o, vel_o, kap_o, sol_o,
    R, S, coef, lhs, flow_v, kap_v, th_v, lin_v, pre_v, ab_v, wat_v, lat_v,
    below_v, above_v, kabove_v, thh, vel_v, knext_v, pig, totals, thn_v,
    lsem, osem, small_s, small_r, hs, hr, fs, fr, vs, vr, bs, br, ps, ts, tr_,
):
    c = lax.axis_index("col")
    s = lax.axis_index("sec")
    left, right = (c + COLS - 1) % COLS, (c + 1) % COLS
    up, down = (s + SECS - 1) % SECS, (s + 1) % SECS

    loads = [
        pltpu.make_async_copy(a, b, lsem.at[i])
        for i, (a, b) in enumerate(
            [(flow, flow_v), (kap, kap_v), (th, th_v), (lin, lin_v), (pre, pre_v), (ab, ab_v), (wat, wat_v), (lat, lat_v)]
        )
    ]
    for copy in loads:
        copy.start()

    barrier = pltpu.get_barrier_semaphore()

    def greet(r, _):
        pl.semaphore_signal(barrier, inc=1, device_id=(c, s ^ r), device_id_type=MESH)
        return 0

    lax.fori_loop(1, SECS, greet, 0)
    pl.semaphore_signal(barrier, inc=1, device_id=(left, s), device_id_type=MESH)
    pl.semaphore_signal(barrier, inc=1, device_id=(right, s), device_id_type=MESH)
    pl.semaphore_wait(barrier, SECS + 1)

    def remote(src, dst, send, recv, to):
        return pltpu.make_async_remote_copy(
            src_ref=src, dst_ref=dst, send_sem=send, recv_sem=recv, device_id=to, device_id_type=MESH
        )

    smalls = [
        remote(flow.at[:, 0], below_v, small_s.at[0], small_r.at[0], (c, up)),
        remote(flow.at[:, LEV - 1], above_v, small_s.at[1], small_r.at[1], (c, down)),
        remote(kap.at[LEV - 1], kabove_v, small_s.at[2], small_r.at[2], (c, down)),
        remote(th.at[:, 0, :], thh.at[1, :, 0, :], small_s.at[3], small_r.at[3], (left, s)),
        remote(th.at[:, LON - 1, :], thh.at[0, :, 0, :], small_s.at[4], small_r.at[4], (right, s)),
    ]
    for copy in smalls:
        copy.start()

    def forward(i, _):
        k = lax.select(i == 1, LEV - 1, lax.select(i == 0, 0, i - 1))
        for t in range(2):
            pltpu.make_async_copy(
                x.at[t, LEV * s + k], R.at[k + 1, pl.ds(1, LON), 2 * s + t, :], fr.at[k]
            ).start()

        def peer(r, _):
            d = s ^ r
            for t in range(2):
                remote(
                    x.at[t, LEV * d + k], R.at[k + 1, pl.ds(1, LON), 2 * s + t, :],
                    fs.at[k], fr.at[k], (c, d),
                ).start()
            return 0

        lax.fori_loop(1, SECS, peer, 0)
        return 0

    lax.fori_loop(0, AHEAD, forward, 0)

    for copy in loads:
        copy.wait()
    for copy in smalls:
        copy.wait()

    rot = jnp.broadcast_to(lat_v[0:1, :], (LON, LAT))
    inv = 1.0 + rot * rot
    wet = wat_v[...].astype(F32)
    row = lax.broadcasted_iota(jnp.int32, (LON, LAT), 0)
    lane = lax.broadcasted_iota(jnp.int32, (LON, LAT), 1)

    def turned(u, v):
        return (u + rot * v) / inv, (v - rot * u) / inv

    below_ok = jnp.where(s == SECS - 1, 0.0, 1.0)
    above_ok = jnp.where(s == 0, 0.0, 1.0)
    east_a, north_a = turned(above_v[0], above_v[1])
    east_b, north_b = turned(below_v[0], below_v[1])
    east, north = turned(flow_v[0, 0], flow_v[1, 0])
    shear = (east_a - east) ** 2 + (north_a - north) ** 2
    k_up = (0.5 * kabove_v[...] + 0.5 * shear / (1.0 + shear)) * (VERTICAL_MIX * above_ok) * wet
    for k in range(LEV):
        vel_v[0, k] = east
        vel_v[1, k] = north
        if k < LEV - 1:
            east_n, north_n = turned(flow_v[0, k + 1], flow_v[1, k + 1])
        else:
            east_n, north_n = east_b * below_ok, north_b * below_ok
        shear = (east - east_n) ** 2 + (north - north_n) ** 2
        knext = 0.5 * kap_v[k] + 0.5 * shear / (1.0 + shear)
        knext_v[k] = knext
        k_down = knext * VERTICAL_MIX * wet
        if k == LEV - 1:
            k_down = k_down * below_ok
        coef[k, 0] = (1.0 - 4.0 * MIXING * wet) - k_down - k_up
        coef[k, 1] = (MIXING - MIXING * east) * wet
        coef[k, 2] = (MIXING + MIXING * east) * wet
        coef[k, 3] = (MIXING - MIXING * north) * wet
        coef[k, 4] = (MIXING + MIXING * north) * wet
        coef[k, 5] = k_down
        coef[k, 6] = k_up
        f = th_v[k]
        f_e = jnp.where(row == LON - 1, jnp.broadcast_to(thh[1, k, 0:1, :], (LON, LAT)), pltpu.roll(f, LON - 1, 0))
        f_w = jnp.where(row == 0, jnp.broadcast_to(thh[0, k, 0:1, :], (LON, LAT)), pltpu.roll(f, 1, 0))
        f_n = jnp.where(lane == LAT - 1, f, pltpu.roll(f, LAT - 1, 1))
        f_s = jnp.where(lane == 0, f, pltpu.roll(f, 1, 1))
        thn_v[k] = (
            f + MIXING * (f_e + f_w + f_n + f_s - 4.0 * f)
            - MIXING * (east * (f_e - f_w) + north * (f_n - f_s))
        )
        east, north, k_up = east_n, north_n, k_down
    outs = [pltpu.make_async_copy(vel_v, vel_o, osem.at[0]), pltpu.make_async_copy(knext_v, kap_o, osem.at[1])]
    for copy in outs:
        copy.start()

    inner = jnp.dot(pre_v[...], lin_v[...], precision=HIGHEST, preferred_element_type=F32)
    scaled = pre_v[...] * ab_v[...]
    at = lax.broadcasted_iota(jnp.int32, (TR, LAT), 1)
    which = lax.broadcasted_iota(jnp.int32, (TR, LAT), 0)
    pick_m = (at % (2 * TR) == which).astype(F32)
    pick_s = (at % (2 * TR) == which + TR).astype(F32)
    first = jnp.dot(inner, pick_m, precision=HIGHEST, preferred_element_type=F32) - jnp.dot(
        scaled, pick_s, precision=HIGHEST, preferred_element_type=F32
    )
    second = -jnp.dot(pre_v[...], first, precision=HIGHEST, preferred_element_type=F32)
    for i, rows in enumerate((first, second)):
        high = rows.astype(BF16)
        low = rows - high.astype(F32)
        lhs[pl.ds(TR * i, TR), :] = jnp.where(at < 4 * TR, high.astype(F32), low).astype(BF16)

    def all_of(k, sem):
        pltpu.make_async_copy(R.at[k + 1, pl.ds(1, LON)], R.at[k + 1, pl.ds(1, LON)], sem).wait()

    verticals = [
        remote(R.at[1, pl.ds(1, LON)], R.at[LEV + 1, pl.ds(1, LON)], vs.at[0], vr.at[0], (c, up)),
        remote(R.at[LEV, pl.ds(1, LON)], R.at[0, pl.ds(1, LON)], vs.at[1], vr.at[1], (c, down)),
    ]

    def arrived(i, _):
        k = lax.select(i == 1, LEV - 1, lax.select(i == 0, 0, i - 1))
        all_of(k, fr.at[k])
        remote(R.at[k + 1, 1], R.at[k + 1, LON + 1], hs, hr.at[k], (left, s)).start()
        remote(R.at[k + 1, LON], R.at[k + 1, 0], hs, hr.at[k], (right, s)).start()

        @pl.when(i == 0)
        def _():
            verticals[0].start()

        @pl.when(i == 1)
        def _():
            verticals[1].start()

        @pl.when(i < LEV - AHEAD)
        def _():
            forward(i + AHEAD, 0)

        return 0

    edge = R.at[pl.ds(1, LEV), pl.ds(0, 2)]
    lax.fori_loop(0, 4, arrived, 0)

    tlane = lax.broadcasted_iota(jnp.int32, (TR, LAT), 1)

    def level(i, _):
        k = lax.select(i == LEV - 1, LEV - 1, lax.select(i == LEV - 2, 0, i + 1))

        @pl.when(i < LEV - 4)
        def _():
            arrived(i + 4, 0)

        both = R.at[k + 1, pl.ds(0, 2)]
        pltpu.make_async_copy(both, both, hr.at[k]).wait()

        @pl.when(i == LEV - 2)
        def _():
            verticals[1].wait_recv()

        @pl.when(i == LEV - 1)
        def _():
            verticals[0].wait_recv()

        def column(j, _):
            def row_of(n):
                return jnp.broadcast_to(coef[k, n, pl.ds(j, 1), :], (TR, LAT))

            center = R[k + 1, j + 1]
            moved = row_of(0) * center
            moved += row_of(1) * R[k + 1, j + 2]
            moved += row_of(2) * R[k + 1, j]
            moved += row_of(3) * jnp.where(tlane == LAT - 1, center, pltpu.roll(center, LAT - 1, 1))
            moved += row_of(4) * jnp.where(tlane == 0, center, pltpu.roll(center, 1, 1))
            moved += row_of(5) * R[k + 2, j + 1]
            moved += row_of(6) * R[k, j + 1]
            y = jnp.dot(lhs[...], stacked_halves(moved, saturating(moved)), preferred_element_type=F32)
            current = moved + y[:TR]
            base = current + y[TR:]
            y = jnp.dot(lhs[:TR, :], stacked_halves(current, saturating(current)), preferred_element_type=F32)
            wet_row = jnp.broadcast_to(wat_v[pl.ds(j, 1), :], (TR, LAT))
            S[k, j] = jnp.where(wet_row > 0, base + y, moved)
            return 0

        lax.fori_loop(0, LON, column, 0, unroll=2)

        pltpu.make_async_copy(S.at[k, :, 0, :], pig.at[k], ps).start()
        for t in range(2):
            pltpu.make_async_copy(S.at[k, :, 2 * s + t, :], sol_o.at[t, LEV * s + k], br.at[k]).start()

        def peer(r, _):
            d = s ^ r
            for t in range(2):
                remote(
                    S.at[k, :, 2 * d + t, :], sol_o.at[t, LEV * s + k], bs.at[k], br.at[k], (c, d)
                ).start()
            return 0

        lax.fori_loop(1, SECS, peer, 0)
        return 0

    lax.fori_loop(0, LEV, level, 0)

    pltpu.make_async_copy(pig, pig, ps).wait()
    total = jnp.zeros((LON, LAT), F32)
    for k in range(LEV):
        total += WATER_ABSORB + PIGMENT_ABSORB * saturating(pig[k])
    totals[s] = total

    def tell(r, _):
        remote(totals.at[s], totals.at[s], ts, tr_, (c, s ^ r)).start()
        return 0

    lax.fori_loop(1, SECS, tell, 0)
    others = totals.at[pl.ds(0, SECS - 1)]
    pltpu.make_async_copy(others, others, tr_).wait()
    depth = jnp.zeros((LON, LAT), F32)
    for d in range(SECS):
        depth += totals[d] * jnp.where(d < s, 1.0, 0.0)
    light = CHLOROPHYLL_WARM * jnp.broadcast_to(lat_v[1:2, :], (LON, LAT)) * wet
    before = jnp.exp(-depth)
    for k in range(LEV):
        depth = depth + (WATER_ABSORB + PIGMENT_ABSORB * saturating(pig[k]))
        after = jnp.exp(-depth)
        thn_v[k] = thn_v[k] + light * (before - after)
        before = after
    outs.append(pltpu.make_async_copy(thn_v, th_o, osem.at[2]))
    outs[-1].start()

    pltpu.make_async_copy(others, others, ts).wait()
    pltpu.make_async_copy(edge, edge, hs).wait()
    for copy in verticals:
        copy.wait_send()
    sent = R.at[1, pl.ds(1, LON - 1)]

    def finish(k, _):
        pltpu.make_async_copy(sent, sent, fs.at[k]).wait()
        pltpu.make_async_copy(sent, sent, bs.at[k]).wait()
        back = sol_o.at[0, pl.ds(0, 2 * SECS)]
        pltpu.make_async_copy(back, back, br.at[k]).wait()
        return 0

    lax.fori_loop(0, LEV, finish, 0)
    for copy in outs:
        copy.wait()


def settle(*refs):
    given, made, sem = refs[:4], refs[4:8], refs[8]
    copies = [pltpu.make_async_copy(a, b, sem.at[i]) for i, (a, b) in enumerate(zip(given, made))]
    for copy in copies:
        copy.start()
    for copy in copies:
        copy.wait()


def on_device(thermal, flow, spreading, solute, lin, pre, ab, water):
    index = (np.arange(LAT, dtype=np.float64) + 0.5) * np.pi / LAT - np.pi / 2
    table = np.zeros((8, LAT), np.float32)
    table[0] = CORIOLIS * np.sin(index)
    table[1] = np.cos(index)
    hbm = pl.BlockSpec(memory_space=pltpu.HBM)
    dma = pltpu.SemaphoreType.DMA
    shapes = tuple(
        jax.ShapeDtypeStruct(a.shape, F32) for a in (thermal, flow, spreading, solute)
    )
    vmem = pl.BlockSpec(memory_space=pltpu.VMEM)
    given = (solute, flow, spreading, thermal, lin, pre, ab.reshape(1, TR), water, jnp.asarray(table))
    results = pl.pallas_call(
        kernel,
        out_shape=shapes,
        in_specs=[hbm] * 9,
        out_specs=(vmem,) * 4,
        scratch_shapes=[
            pltpu.VMEM((LEV + 2, LON + 2, TR, LAT), F32),
            pltpu.VMEM((LEV, LON, TR, LAT), F32),
            pltpu.VMEM((LEV, 7, LON, LAT), F32),
            pltpu.VMEM((2 * TR, LAT), BF16),
            pltpu.VMEM((2, LEV, LON, LAT), F32),
            pltpu.VMEM((LEV, LON, LAT), F32),
            pltpu.VMEM((LEV, LON, LAT), F32),
            pltpu.VMEM((TR, TR), F32),
            pltpu.VMEM((TR, TR), F32),
            pltpu.VMEM((1, TR), F32),
            pltpu.VMEM((LON, LAT), jnp.int32),
            pltpu.VMEM((8, LAT), F32),
            pltpu.VMEM((2, LON, LAT), F32),
            pltpu.VMEM((2, LON, LAT), F32),
            pltpu.VMEM((LON, LAT), F32),
            pltpu.VMEM((2, LEV, 8, LAT), F32),
            pltpu.VMEM((2, LEV, LON, LAT), F32),
            pltpu.VMEM((LEV, LON, LAT), F32),
            pltpu.VMEM((LEV, LON, LAT), F32),
            pltpu.VMEM((SECS, LON, LAT), F32),
            pltpu.VMEM((LEV, LON, LAT), F32),
            dma((8,)), dma((3,)), dma((5,)), dma((5,)),
            dma, dma((LEV,)), dma((LEV,)), dma((LEV,)), dma((2,)), dma((2,)), dma((LEV,)), dma((LEV,)),
            dma, dma, dma,
        ],
        compiler_params=pltpu.CompilerParams(
            collective_id=0, has_side_effects=True, vmem_limit_bytes=28 << 20
        ),
        name="ocean_step",
    )(*(pltpu.with_memory_space_constraint(a, pltpu.HBM) for a in given))
    return pl.pallas_call(
        settle,
        out_shape=shapes,
        in_specs=[vmem] * 4,
        out_specs=(hbm,) * 4,
        scratch_shapes=[dma((4,))],
        compiler_params=pltpu.CompilerParams(vmem_limit_bytes=16 << 20),
        name="settle",
    )(*results)


def solution(mesh):
    placed = (
        P("sec", "col", None),
        P(None, "sec", "col", None),
        P("sec", "col", None),
        P("sec", None, "col", None),
        P(),
        P(),
        P(),
        P("col", None),
    )
    return jax.shard_map(
        on_device,
        mesh=mesh,
        in_specs=placed,
        out_specs=placed[:1] + placed[1:4],
        check_vma=False,
    )
```

```python
import jax
import jax.numpy as jnp
import numpy as np
from jax import lax
from jax.experimental import pallas as pl
from jax.experimental.pallas import tpu as pltpu
from jax.sharding import PartitionSpec as P

CORIOLIS = 0.8
MIXING = 0.1
VERTICAL_MIX = 0.3
WATER_ABSORB = 0.02
PIGMENT_ABSORB = 0.06
CHLOROPHYLL_WARM = 10.0

SECS = 16
COLS = 8
LEV = 8
LON = 16
TR = 32
LAT = 256
AHEAD = 4
KEPT = 12
BITS = 5
HALF = 128
PIECES = LON * LAT // HALF
MESH = pl.DeviceIdType.MESH
F32 = jnp.float32
BF16 = jnp.bfloat16
HIGHEST = lax.Precision.HIGHEST


def saturating(value):
    return 1.0 - 1.0 / (1.0 + value * value)


def stacked_halves(top, bottom):
    both = jnp.concatenate([top, bottom], axis=0)
    high = both.astype(BF16)
    low = (both - high.astype(F32)).astype(BF16)
    return jnp.concatenate([high, low, high, low], axis=0)


def along(piece, index):
    return jnp.take_along_axis(piece, index, axis=1)


def kernel(
    x, flow, kap, th, lin, pre, ab, wat, lat,
    th_o, vel_o, kap_o, sol_o,
    R, S, C, D, comes, goes, gather, scatter, coef, lhs, flow_v, kap_v, th_v, lin_v, pre_v, ab_v, wat_v, lat_v,
    below_v, above_v, kabove_v, thh, vel_v, knext_v, pig, totals, thn_v, scr_v,
    lsem, osem, small_s, small_r, hs, hr, fs, fr, vs, vr, bs, br, ts, tr_, xs,
):
    c = lax.axis_index("col")
    s = lax.axis_index("sec")
    left, right = (c + COLS - 1) % COLS, (c + 1) % COLS
    up, down = (s + SECS - 1) % SECS, (s + 1) % SECS

    loads = [
        pltpu.make_async_copy(a, b, lsem.at[i])
        for i, (a, b) in enumerate(
            [(flow, flow_v), (kap, kap_v), (th, th_v), (lin, lin_v), (pre, pre_v), (ab, ab_v), (wat, wat_v), (lat, lat_v)]
        )
    ]
    for copy in loads:
        copy.start()

    barrier = pltpu.get_barrier_semaphore()

    def greet(r, _):
        pl.semaphore_signal(barrier, inc=1, device_id=(c, s ^ r), device_id_type=MESH)
        return 0

    lax.fori_loop(1, SECS, greet, 0)
    pl.semaphore_signal(barrier, inc=1, device_id=(left, s), device_id_type=MESH)
    pl.semaphore_signal(barrier, inc=1, device_id=(right, s), device_id_type=MESH)
    pl.semaphore_wait(barrier, SECS + 1)

    def remote(src, dst, send, recv, to):
        return pltpu.make_async_remote_copy(
            src_ref=src, dst_ref=dst, send_sem=send, recv_sem=recv, device_id=to, device_id_type=MESH
        )

    smalls = [
        remote(flow.at[:, 0], below_v, small_s.at[0], small_r.at[0], (c, up)),
        remote(flow.at[:, LEV - 1], above_v, small_s.at[1], small_r.at[1], (c, down)),
        remote(kap.at[LEV - 1], kabove_v, small_s.at[2], small_r.at[2], (c, down)),
        remote(th.at[:, 0, :], thh.at[1, :, 0, :], small_s.at[3], small_r.at[3], (left, s)),
        remote(th.at[:, LON - 1, :], thh.at[0, :, 0, :], small_s.at[4], small_r.at[4], (right, s)),
    ]
    for copy in smalls:
        copy.start()

    def forward(i, _):
        k = lax.select(i == 1, LEV - 1, lax.select(i == 0, 0, i - 1))
        for t in range(2):
            pltpu.make_async_copy(
                x.at[t, LEV * s + k], R.at[k + 1, pl.ds(1, LON), 2 * s + t, :], fr.at[k]
            ).start()

        def peer(r, _):
            d = s ^ r
            for t in range(2):
                remote(
                    x.at[t, LEV * d + k], R.at[k + 1, pl.ds(1, LON), 2 * s + t, :],
                    fs.at[k], fr.at[k], (c, d),
                ).start()
            return 0

        lax.fori_loop(1, SECS, peer, 0)
        return 0

    lax.fori_loop(0, AHEAD, forward, 0)

    original = pltpu.make_async_copy(x, sol_o, xs)
    original.start()

    for copy in loads:
        copy.wait()
    for copy in smalls:
        copy.wait()

    rot = jnp.broadcast_to(lat_v[0:1, :], (LON, LAT))
    inv = 1.0 + rot * rot
    wet = wat_v[...].astype(F32)
    row = lax.broadcasted_iota(jnp.int32, (LON, LAT), 0)
    lane = lax.broadcasted_iota(jnp.int32, (LON, LAT), 1)

    def turned(u, v):
        return (u + rot * v) / inv, (v - rot * u) / inv

    below_ok = jnp.where(s == SECS - 1, 0.0, 1.0)
    above_ok = jnp.where(s == 0, 0.0, 1.0)
    east_a, north_a = turned(above_v[0], above_v[1])
    east_b, north_b = turned(below_v[0], below_v[1])
    east, north = turned(flow_v[0, 0], flow_v[1, 0])
    shear = (east_a - east) ** 2 + (north_a - north) ** 2
    k_up = (0.5 * kabove_v[...] + 0.5 * shear / (1.0 + shear)) * (VERTICAL_MIX * above_ok) * wet
    for k in range(LEV):
        vel_v[0, k] = east
        vel_v[1, k] = north
        if k < LEV - 1:
            east_n, north_n = turned(flow_v[0, k + 1], flow_v[1, k + 1])
        else:
            east_n, north_n = east_b * below_ok, north_b * below_ok
        shear = (east - east_n) ** 2 + (north - north_n) ** 2
        knext = 0.5 * kap_v[k] + 0.5 * shear / (1.0 + shear)
        knext_v[k] = knext
        k_down = knext * VERTICAL_MIX * wet
        if k == LEV - 1:
            k_down = k_down * below_ok
        coef[k, 0] = (1.0 - 4.0 * MIXING * wet) - k_down - k_up
        coef[k, 1] = (MIXING - MIXING * east) * wet
        coef[k, 2] = (MIXING + MIXING * east) * wet
        coef[k, 3] = (MIXING - MIXING * north) * wet
        coef[k, 4] = (MIXING + MIXING * north) * wet
        coef[k, 5] = k_down
        coef[k, 6] = k_up
        f = th_v[k]
        f_e = jnp.where(row == LON - 1, jnp.broadcast_to(thh[1, k, 0:1, :], (LON, LAT)), pltpu.roll(f, LON - 1, 0))
        f_w = jnp.where(row == 0, jnp.broadcast_to(thh[0, k, 0:1, :], (LON, LAT)), pltpu.roll(f, 1, 0))
        f_n = jnp.where(lane == LAT - 1, f, pltpu.roll(f, LAT - 1, 1))
        f_s = jnp.where(lane == 0, f, pltpu.roll(f, 1, 1))
        thn_v[k] = (
            f + MIXING * (f_e + f_w + f_n + f_s - 4.0 * f)
            - MIXING * (east * (f_e - f_w) + north * (f_n - f_s))
        )
        east, north, k_up = east_n, north_n, k_down
    outs = [pltpu.make_async_copy(vel_v, vel_o, osem.at[0]), pltpu.make_async_copy(knext_v, kap_o, osem.at[1])]
    for copy in outs:
        copy.start()

    inner = jnp.dot(pre_v[...], lin_v[...], precision=HIGHEST, preferred_element_type=F32)
    scaled = pre_v[...] * ab_v[...]
    at = lax.broadcasted_iota(jnp.int32, (TR, LAT), 1)
    which = lax.broadcasted_iota(jnp.int32, (TR, LAT), 0)
    pick_m = (at % (2 * TR) == which).astype(F32)
    pick_s = (at % (2 * TR) == which + TR).astype(F32)
    first = jnp.dot(inner, pick_m, precision=HIGHEST, preferred_element_type=F32) - jnp.dot(
        scaled, pick_s, precision=HIGHEST, preferred_element_type=F32
    )
    second = -jnp.dot(pre_v[...], first, precision=HIGHEST, preferred_element_type=F32)
    for i, rows in enumerate((first, second)):
        high = rows.astype(BF16)
        low = rows - high.astype(F32)
        lhs[pl.ds(TR * i, TR), :] = jnp.where(at < 4 * TR, high.astype(F32), low).astype(BF16)

    lane8 = lax.broadcasted_iota(jnp.int32, (8, HALF), 1)
    wide = lax.broadcasted_iota(jnp.int32, (LAT, LAT), 0)
    wide_t = lax.broadcasted_iota(jnp.int32, (LAT, LAT), 1)
    same = wide // HALF == wide_t // HALF
    ahead_of = jnp.where(same & (wide < wide_t), 1.0, 0.0).astype(BF16)
    beside = jnp.where(same, 1.0, 0.0).astype(BF16)
    left_of = jnp.where(wide // HALF < wide_t // HALF, 1.0, 0.0).astype(BF16)
    row_t = lax.broadcasted_iota(jnp.int32, (LON, LON), 1)
    rows_before = jnp.where(lax.broadcasted_iota(jnp.int32, (LON, LON), 0) > row_t, 1.0, 0.0).astype(BF16)
    wet_b = wet.astype(BF16)
    rank = jnp.dot(wet_b, ahead_of, preferred_element_type=F32)
    before = jnp.dot(rows_before, wet_b, preferred_element_type=F32)
    before = jnp.dot(before.astype(BF16), jnp.ones((LAT, LAT), BF16), preferred_element_type=F32)
    before = before + jnp.dot(wet_b, left_of, preferred_element_type=F32)
    tables = [rank, before, jnp.dot(wet_b, beside, preferred_element_type=F32), wet]
    for i, table in enumerate(tables):
        scr_v[i] = table.astype(jnp.int32)

    def piece_of(i, v):
        part = scr_v[i, v // 2 : v // 2 + 1, (v % 2) * HALF : (v % 2 + 1) * HALF]
        return jnp.broadcast_to(part, (8, HALF))

    shift = []
    for v in range(PIECES):
        ranks, start, count, is_wet = (piece_of(i, v) for i in range(4))
        scatter[v] = (start + ranks) & (HALF - 1)
        lanes, moves = lane8, jnp.where(is_wet > 0, lane8 - ranks, 0)
        for bit in range(7):
            by = 1 << bit
            inside = lane8 < HALF - by
            next_m = jnp.where(inside, pltpu.roll(moves, HALF - by, 1), 0)
            enters = (next_m & by) > 0
            lanes = jnp.where(enters, pltpu.roll(lanes, HALF - by, 1), lanes)
            moves = jnp.where(enters, next_m, jnp.where((moves & by) > 0, 0, moves))
        turn = (lane8 - start) & (HALF - 1)
        gather[v] = along(lanes, turn)
        shift.append(jnp.where(turn < count, v - ((start + turn) >> 7), 0))
    for bit in range(BITS):
        far = 1 << bit
        for v in range(PIECES):
            leaves = (shift[v] >> bit) & 1
            goes[bit * PIECES + v] = leaves
            if v + far < PIECES:
                enters = (shift[v + far] >> bit) & 1
                comes[bit * PIECES + v] = enters
                shift[v] = jnp.where(enters > 0, shift[v + far], jnp.where(leaves > 0, 0, shift[v]))
            else:
                shift[v] = jnp.where(leaves > 0, 0, shift[v])

    def all_of(k, sem):
        pltpu.make_async_copy(R.at[k + 1, pl.ds(1, LON)], R.at[k + 1, pl.ds(1, LON)], sem).wait()

    verticals = [
        remote(R.at[1, pl.ds(1, LON)], R.at[LEV + 1, pl.ds(1, LON)], vs.at[0], vr.at[0], (c, up)),
        remote(R.at[LEV, pl.ds(1, LON)], R.at[0, pl.ds(1, LON)], vs.at[1], vr.at[1], (c, down)),
    ]

    def arrived(i, _):
        k = lax.select(i == 1, LEV - 1, lax.select(i == 0, 0, i - 1))
        all_of(k, fr.at[k])
        remote(R.at[k + 1, 1], R.at[k + 1, LON + 1], hs, hr.at[k], (left, s)).start()
        remote(R.at[k + 1, LON], R.at[k + 1, 0], hs, hr.at[k], (right, s)).start()

        @pl.when(i == 0)
        def _():
            verticals[0].start()

        @pl.when(i == 1)
        def _():
            verticals[1].start()

        @pl.when(i < LEV - AHEAD)
        def _():
            forward(i + AHEAD, 0)

        return 0

    edge = R.at[pl.ds(1, LEV), pl.ds(0, 2)]
    lax.fori_loop(0, 4, arrived, 0)

    tlane = lax.broadcasted_iota(jnp.int32, (TR, LAT), 1)

    def level(i, _):
        k = lax.select(i == LEV - 1, LEV - 1, lax.select(i == LEV - 2, 0, i + 1))

        both = R.at[k + 1, pl.ds(0, 2)]
        pltpu.make_async_copy(both, both, hr.at[k]).wait()

        @pl.when(i == LEV - 2)
        def _():
            verticals[1].wait_recv()

        @pl.when(i == LEV - 1)
        def _():
            verticals[0].wait_recv()

        def column(j, _):
            def row_of(n):
                return jnp.broadcast_to(coef[k, n, pl.ds(j, 1), :], (TR, LAT))

            center = R[k + 1, j + 1]
            moved = row_of(0) * center
            moved += row_of(1) * R[k + 1, j + 2]
            moved += row_of(2) * R[k + 1, j]
            moved += row_of(3) * jnp.where(tlane == LAT - 1, center, pltpu.roll(center, LAT - 1, 1))
            moved += row_of(4) * jnp.where(tlane == 0, center, pltpu.roll(center, 1, 1))
            moved += row_of(5) * R[k + 2, j + 1]
            moved += row_of(6) * R[k, j + 1]
            y = jnp.dot(lhs[...], stacked_halves(moved, saturating(moved)), preferred_element_type=F32)
            current = moved + y[:TR]
            base = current + y[TR:]
            y = jnp.dot(lhs[:TR, :], stacked_halves(current, saturating(current)), preferred_element_type=F32)
            wet_row = jnp.broadcast_to(wat_v[pl.ds(j, 1), :], (TR, LAT))
            reacted = jnp.where(wet_row > 0, base + y, moved)
            S[j] = reacted
            pig[k, pl.ds(j, 1), :] = reacted[0:1]
            return 0

        lax.fori_loop(0, LON, column, 0, unroll=2)

        @pl.when(i < LEV - 4)
        def _():
            arrived(i + 4, 0)

        def pack(g, _):
            pieces = [
                along(S[v // 2, pl.ds(8 * g, 8), (v % 2) * HALF : (v % 2 + 1) * HALF], gather[v])
                for v in range(PIECES)
            ]
            for bit in range(BITS):
                far = 1 << bit
                for v in range(PIECES - far):
                    pieces[v] = jnp.where(comes[bit * PIECES + v] > 0, pieces[v + far], pieces[v])
            for v in range(2 * KEPT):
                C[k, v // 2, pl.ds(8 * g, 8), (v % 2) * HALF : (v % 2 + 1) * HALF] = pieces[v]
            return 0

        lax.fori_loop(0, TR // 8, pack, 0)

        for t in range(2):
            pltpu.make_async_copy(C.at[k, :, 2 * s + t, :], D.at[k, t, :, s, :], br.at[k]).start()

        def peer(r, _):
            d = s ^ r
            for t in range(2):
                remote(
                    C.at[k, :, 2 * d + t, :], D.at[k, t, :, s, :], bs.at[k], br.at[k], (c, d)
                ).start()
            return 0

        lax.fori_loop(1, SECS, peer, 0)

        return 0

    lax.fori_loop(0, LEV, level, 0)

    total = jnp.zeros((LON, LAT), F32)
    for k in range(LEV):
        total += WATER_ABSORB + PIGMENT_ABSORB * saturating(pig[k])
    totals[s] = total

    def tell(r, _):
        remote(totals.at[s], totals.at[s], ts, tr_, (c, s ^ r)).start()
        return 0

    lax.fori_loop(1, SECS, tell, 0)
    others = totals.at[pl.ds(0, SECS - 1)]
    pltpu.make_async_copy(others, others, tr_).wait()
    depth = jnp.zeros((LON, LAT), F32)
    for d in range(SECS):
        depth += totals[d] * jnp.where(d < s, 1.0, 0.0)
    light = CHLOROPHYLL_WARM * jnp.broadcast_to(lat_v[1:2, :], (LON, LAT)) * wet
    before = jnp.exp(-depth)
    for k in range(LEV):
        depth = depth + (WATER_ABSORB + PIGMENT_ABSORB * saturating(pig[k]))
        after = jnp.exp(-depth)
        thn_v[k] = thn_v[k] + light * (before - after)
        before = after
    outs.append(pltpu.make_async_copy(thn_v, th_o, osem.at[2]))
    outs[-1].start()

    pltpu.make_async_copy(others, others, ts).wait()
    pltpu.make_async_copy(edge, edge, hs).wait()
    for copy in verticals:
        copy.wait_send()
    sent = R.at[1, pl.ds(1, LON - 1)]

    def receive(i, _):
        k = lax.select(i == LEV - 1, LEV - 1, lax.select(i == LEV - 2, 0, i + 1))
        pltpu.make_async_copy(D.at[k], D.at[k], br.at[k]).wait()

        def unpack(n, _):
            t, half = n // 2, n % 2
            pieces = [
                D[k, t, v // 2, pl.ds(8 * half, 8), (v % 2) * HALF : (v % 2 + 1) * HALF]
                for v in range(2 * KEPT)
            ]
            pieces += [pieces[-1]] * (PIECES - 2 * KEPT)
            for bit in reversed(range(BITS)):
                far = 1 << bit
                for v in reversed(range(far, PIECES)):
                    pieces[v] = jnp.where(goes[bit * PIECES + v] > 0, pieces[v - far], pieces[v])
            pieces = [along(pieces[v], scatter[v]) for v in range(PIECES)]
            for group in range(2):
                for side in range(2):
                    lanes = slice(side * HALF, (side + 1) * HALF)
                    block = jnp.stack([pieces[2 * (8 * group + j) + side] for j in range(8)])
                    block = jnp.swapaxes(block, 0, 1)
                    here = wat_v[8 * group : 8 * group + 8, lanes] > 0
                    for d in range(8):
                        at = (t, LEV * (8 * half + d) + k, pl.ds(8 * group, 8), lanes)
                        sol_o[at] = jnp.where(here, block[d], sol_o[at])
            return 0

        lax.fori_loop(0, 4, unpack, 0)
        return 0

    original.wait()
    lax.fori_loop(0, LEV, receive, 0)
    packed = goes.at[pl.ds(0, 2 * (SECS - 1) * KEPT * LAT // (8 * HALF))]

    def finish(k, _):
        pltpu.make_async_copy(sent, sent, fs.at[k]).wait()
        pltpu.make_async_copy(packed, packed, bs.at[k]).wait()
        return 0

    lax.fori_loop(0, LEV, finish, 0)
    for copy in outs:
        copy.wait()


def settle(*refs):
    given, made, sem = refs[:4], refs[4:8], refs[8]
    copies = [pltpu.make_async_copy(a, b, sem.at[i]) for i, (a, b) in enumerate(zip(given, made))]
    for copy in copies:
        copy.start()
    for copy in copies:
        copy.wait()


def on_device(thermal, flow, spreading, solute, lin, pre, ab, water):
    index = (np.arange(LAT, dtype=np.float64) + 0.5) * np.pi / LAT - np.pi / 2
    table = np.zeros((8, LAT), np.float32)
    table[0] = CORIOLIS * np.sin(index)
    table[1] = np.cos(index)
    hbm = pl.BlockSpec(memory_space=pltpu.HBM)
    dma = pltpu.SemaphoreType.DMA
    shapes = tuple(
        jax.ShapeDtypeStruct(a.shape, F32) for a in (thermal, flow, spreading, solute)
    )
    vmem = pl.BlockSpec(memory_space=pltpu.VMEM)
    given = (solute, flow, spreading, thermal, lin, pre, ab.reshape(1, TR), water, jnp.asarray(table))
    results = pl.pallas_call(
        kernel,
        out_shape=shapes,
        in_specs=[hbm] * 9,
        out_specs=(vmem,) * 4,
        scratch_shapes=[
            pltpu.VMEM((LEV + 2, LON + 2, TR, LAT), F32),
            pltpu.VMEM((LON, TR, LAT), F32),
            pltpu.VMEM((LEV, KEPT, TR, LAT), F32),
            pltpu.VMEM((LEV, 2, KEPT, SECS, LAT), F32),
            pltpu.VMEM((BITS * PIECES, 8, HALF), jnp.int32),
            pltpu.VMEM((BITS * PIECES, 8, HALF), jnp.int32),
            pltpu.VMEM((PIECES, 8, HALF), jnp.int32),
            pltpu.VMEM((PIECES, 8, HALF), jnp.int32),
            pltpu.VMEM((LEV, 7, LON, LAT), F32),
            pltpu.VMEM((2 * TR, LAT), BF16),
            pltpu.VMEM((2, LEV, LON, LAT), F32),
            pltpu.VMEM((LEV, LON, LAT), F32),
            pltpu.VMEM((LEV, LON, LAT), F32),
            pltpu.VMEM((TR, TR), F32),
            pltpu.VMEM((TR, TR), F32),
            pltpu.VMEM((1, TR), F32),
            pltpu.VMEM((LON, LAT), jnp.int32),
            pltpu.VMEM((8, LAT), F32),
            pltpu.VMEM((2, LON, LAT), F32),
            pltpu.VMEM((2, LON, LAT), F32),
            pltpu.VMEM((LON, LAT), F32),
            pltpu.VMEM((2, LEV, 8, LAT), F32),
            pltpu.VMEM((2, LEV, LON, LAT), F32),
            pltpu.VMEM((LEV, LON, LAT), F32),
            pltpu.VMEM((LEV, LON, LAT), F32),
            pltpu.VMEM((SECS, LON, LAT), F32),
            pltpu.VMEM((LEV, LON, LAT), F32),
            pltpu.VMEM((4, LON, LAT), jnp.int32),
            dma((8,)), dma((3,)), dma((5,)), dma((5,)),
            dma, dma((LEV,)), dma((LEV,)), dma((LEV,)), dma((2,)), dma((2,)), dma((LEV,)), dma((LEV,)),
            dma, dma, dma,
        ],
        compiler_params=pltpu.CompilerParams(
            collective_id=0, has_side_effects=True, vmem_limit_bytes=48 << 20
        ),
        name="ocean_step",
    )(*(pltpu.with_memory_space_constraint(a, pltpu.HBM) for a in given))
    return pl.pallas_call(
        settle,
        out_shape=shapes,
        in_specs=[vmem] * 4,
        out_specs=(hbm,) * 4,
        scratch_shapes=[dma((4,))],
        compiler_params=pltpu.CompilerParams(vmem_limit_bytes=16 << 20),
        name="settle",
    )(*results)


def solution(mesh):
    placed = (
        P("sec", "col", None),
        P(None, "sec", "col", None),
        P("sec", "col", None),
        P("sec", None, "col", None),
        P(),
        P(),
        P(),
        P("col", None),
    )
    return jax.shard_map(
        on_device,
        mesh=mesh,
        in_specs=placed,
        out_specs=placed[:1] + placed[1:4],
        check_vma=False,
    )
```

```python
import jax
import jax.numpy as jnp
import numpy as np
from jax import lax
from jax.experimental import pallas as pl
from jax.experimental.pallas import tpu as pltpu
from jax.sharding import PartitionSpec as P

CORIOLIS = 0.8
MIXING = 0.1
VERTICAL_MIX = 0.3
WATER_ABSORB = 0.02
PIGMENT_ABSORB = 0.06
CHLOROPHYLL_WARM = 10.0

SECS = 16
COLS = 8
LEV = 8
LON = 16
TR = 32
LAT = 256
AHEAD = 4
KEPT = 12
BITS = 5
HALF = 128
PIECES = LON * LAT // HALF
MESH = pl.DeviceIdType.MESH
F32 = jnp.float32
BF16 = jnp.bfloat16
HIGHEST = lax.Precision.HIGHEST


def saturating(value):
    return 1.0 - 1.0 / (1.0 + value * value)


def stacked_halves(top, bottom):
    both = jnp.concatenate([top, bottom], axis=0)
    high = both.astype(BF16)
    low = (both - high.astype(F32)).astype(BF16)
    return jnp.concatenate([high, low, high, low], axis=0)


def along(piece, index):
    return jnp.take_along_axis(piece, index, axis=1)


def kernel(
    x, flow, kap, th, lin, pre, ab, wat, lat,
    th_o, vel_o, kap_o, sol_o,
    R, S, C, D, comes, goes, gather, scatter, coef, lhs, flow_v, kap_v, th_v, lin_v, pre_v, ab_v, wat_v, lat_v,
    below_v, above_v, kabove_v, thh, vel_v, knext_v, pig, totals, thn_v, scr_v,
    lsem, osem, small_s, small_r, hs, hr, fs, fr, vs, vr, bs, br, ts, tr_, xs,
):
    c = lax.axis_index("col")
    s = lax.axis_index("sec")
    left, right = (c + COLS - 1) % COLS, (c + 1) % COLS
    up, down = (s + SECS - 1) % SECS, (s + 1) % SECS

    loads = [
        pltpu.make_async_copy(a, b, lsem.at[i])
        for i, (a, b) in enumerate(
            [(flow, flow_v), (kap, kap_v), (th, th_v), (lin, lin_v), (pre, pre_v), (ab, ab_v), (wat, wat_v), (lat, lat_v)]
        )
    ]
    for copy in loads:
        copy.start()

    barrier = pltpu.get_barrier_semaphore()

    def greet(r, _):
        pl.semaphore_signal(barrier, inc=1, device_id=(c, s ^ r), device_id_type=MESH)
        return 0

    lax.fori_loop(1, SECS, greet, 0)
    pl.semaphore_signal(barrier, inc=1, device_id=(left, s), device_id_type=MESH)
    pl.semaphore_signal(barrier, inc=1, device_id=(right, s), device_id_type=MESH)
    pl.semaphore_wait(barrier, SECS + 1)

    def remote(src, dst, send, recv, to):
        return pltpu.make_async_remote_copy(
            src_ref=src, dst_ref=dst, send_sem=send, recv_sem=recv, device_id=to, device_id_type=MESH
        )

    smalls = [
        remote(flow.at[:, 0], below_v, small_s.at[0], small_r.at[0], (c, up)),
        remote(flow.at[:, LEV - 1], above_v, small_s.at[1], small_r.at[1], (c, down)),
        remote(kap.at[LEV - 1], kabove_v, small_s.at[2], small_r.at[2], (c, down)),
        remote(th.at[:, 0, :], thh.at[1, :, 0, :], small_s.at[3], small_r.at[3], (left, s)),
        remote(th.at[:, LON - 1, :], thh.at[0, :, 0, :], small_s.at[4], small_r.at[4], (right, s)),
    ]
    for copy in smalls:
        copy.start()

    def forward(i, _):
        k = lax.select(i == 1, LEV - 1, lax.select(i == 0, 0, i - 1))
        for t in range(2):
            pltpu.make_async_copy(
                x.at[t, LEV * s + k], R.at[k + 1, pl.ds(1, LON), 2 * s + t, :], fr.at[k]
            ).start()

        def peer(r, _):
            d = (s + r) % SECS
            for t in range(2):
                remote(
                    x.at[t, LEV * d + k], R.at[k + 1, pl.ds(1, LON), 2 * s + t, :],
                    fs.at[k], fr.at[k], (c, d),
                ).start()
            return 0

        lax.fori_loop(1, SECS, peer, 0)
        return 0

    lax.fori_loop(0, AHEAD, forward, 0)

    original = pltpu.make_async_copy(x, sol_o, xs)
    original.start()

    for copy in loads:
        copy.wait()
    for copy in smalls:
        copy.wait()

    rot = jnp.broadcast_to(lat_v[0:1, :], (LON, LAT))
    inv = 1.0 + rot * rot
    wet = wat_v[...].astype(F32)
    row = lax.broadcasted_iota(jnp.int32, (LON, LAT), 0)
    lane = lax.broadcasted_iota(jnp.int32, (LON, LAT), 1)

    def turned(u, v):
        return (u + rot * v) / inv, (v - rot * u) / inv

    below_ok = jnp.where(s == SECS - 1, 0.0, 1.0)
    above_ok = jnp.where(s == 0, 0.0, 1.0)
    east_a, north_a = turned(above_v[0], above_v[1])
    east_b, north_b = turned(below_v[0], below_v[1])
    east, north = turned(flow_v[0, 0], flow_v[1, 0])
    shear = (east_a - east) ** 2 + (north_a - north) ** 2
    k_up = (0.5 * kabove_v[...] + 0.5 * shear / (1.0 + shear)) * (VERTICAL_MIX * above_ok) * wet
    for k in range(LEV):
        vel_v[0, k] = east
        vel_v[1, k] = north
        if k < LEV - 1:
            east_n, north_n = turned(flow_v[0, k + 1], flow_v[1, k + 1])
        else:
            east_n, north_n = east_b * below_ok, north_b * below_ok
        shear = (east - east_n) ** 2 + (north - north_n) ** 2
        knext = 0.5 * kap_v[k] + 0.5 * shear / (1.0 + shear)
        knext_v[k] = knext
        k_down = knext * VERTICAL_MIX * wet
        if k == LEV - 1:
            k_down = k_down * below_ok
        coef[k, 0] = (1.0 - 4.0 * MIXING * wet) - k_down - k_up
        coef[k, 1] = (MIXING - MIXING * east) * wet
        coef[k, 2] = (MIXING + MIXING * east) * wet
        coef[k, 3] = (MIXING - MIXING * north) * wet
        coef[k, 4] = (MIXING + MIXING * north) * wet
        coef[k, 5] = k_down
        coef[k, 6] = k_up
        f = th_v[k]
        f_e = jnp.where(row == LON - 1, jnp.broadcast_to(thh[1, k, 0:1, :], (LON, LAT)), pltpu.roll(f, LON - 1, 0))
        f_w = jnp.where(row == 0, jnp.broadcast_to(thh[0, k, 0:1, :], (LON, LAT)), pltpu.roll(f, 1, 0))
        f_n = jnp.where(lane == LAT - 1, f, pltpu.roll(f, LAT - 1, 1))
        f_s = jnp.where(lane == 0, f, pltpu.roll(f, 1, 1))
        thn_v[k] = (
            f + MIXING * (f_e + f_w + f_n + f_s - 4.0 * f)
            - MIXING * (east * (f_e - f_w) + north * (f_n - f_s))
        )
        east, north, k_up = east_n, north_n, k_down
    outs = [pltpu.make_async_copy(vel_v, vel_o, osem.at[0]), pltpu.make_async_copy(knext_v, kap_o, osem.at[1])]
    for copy in outs:
        copy.start()

    inner = jnp.dot(pre_v[...], lin_v[...], precision=HIGHEST, preferred_element_type=F32)
    scaled = pre_v[...] * ab_v[...]
    at = lax.broadcasted_iota(jnp.int32, (TR, LAT), 1)
    which = lax.broadcasted_iota(jnp.int32, (TR, LAT), 0)
    pick_m = (at % (2 * TR) == which).astype(F32)
    pick_s = (at % (2 * TR) == which + TR).astype(F32)
    first = jnp.dot(inner, pick_m, precision=HIGHEST, preferred_element_type=F32) - jnp.dot(
        scaled, pick_s, precision=HIGHEST, preferred_element_type=F32
    )
    second = -jnp.dot(pre_v[...], first, precision=HIGHEST, preferred_element_type=F32)
    for i, rows in enumerate((first, second)):
        high = rows.astype(BF16)
        low = rows - high.astype(F32)
        lhs[pl.ds(TR * i, TR), :] = jnp.where(at < 4 * TR, high.astype(F32), low).astype(BF16)

    lane8 = lax.broadcasted_iota(jnp.int32, (8, HALF), 1)
    wide = lax.broadcasted_iota(jnp.int32, (LAT, LAT), 0)
    wide_t = lax.broadcasted_iota(jnp.int32, (LAT, LAT), 1)
    same = wide // HALF == wide_t // HALF
    ahead_of = jnp.where(same & (wide < wide_t), 1.0, 0.0).astype(BF16)
    beside = jnp.where(same, 1.0, 0.0).astype(BF16)
    left_of = jnp.where(wide // HALF < wide_t // HALF, 1.0, 0.0).astype(BF16)
    row_t = lax.broadcasted_iota(jnp.int32, (LON, LON), 1)
    rows_before = jnp.where(lax.broadcasted_iota(jnp.int32, (LON, LON), 0) > row_t, 1.0, 0.0).astype(BF16)
    wet_b = wet.astype(BF16)
    rank = jnp.dot(wet_b, ahead_of, preferred_element_type=F32)
    before = jnp.dot(rows_before, wet_b, preferred_element_type=F32)
    before = jnp.dot(before.astype(BF16), jnp.ones((LAT, LAT), BF16), preferred_element_type=F32)
    before = before + jnp.dot(wet_b, left_of, preferred_element_type=F32)
    tables = [rank, before, jnp.dot(wet_b, beside, preferred_element_type=F32), wet]
    for i, table in enumerate(tables):
        scr_v[i] = table.astype(jnp.int32)

    def piece_of(i, v):
        part = scr_v[i, v // 2 : v // 2 + 1, (v % 2) * HALF : (v % 2 + 1) * HALF]
        return jnp.broadcast_to(part, (8, HALF))

    shift = []
    for v in range(PIECES):
        ranks, start, count, is_wet = (piece_of(i, v) for i in range(4))
        scatter[v] = (start + ranks) & (HALF - 1)
        lanes, moves = lane8, jnp.where(is_wet > 0, lane8 - ranks, 0)
        for bit in range(7):
            by = 1 << bit
            inside = lane8 < HALF - by
            next_m = jnp.where(inside, pltpu.roll(moves, HALF - by, 1), 0)
            enters = (next_m & by) > 0
            lanes = jnp.where(enters, pltpu.roll(lanes, HALF - by, 1), lanes)
            moves = jnp.where(enters, next_m, jnp.where((moves & by) > 0, 0, moves))
        turn = (lane8 - start) & (HALF - 1)
        gather[v] = along(lanes, turn)
        shift.append(jnp.where(turn < count, v - ((start + turn) >> 7), 0))
    for bit in range(BITS):
        far = 1 << bit
        for v in range(PIECES):
            leaves = (shift[v] >> bit) & 1
            goes[bit * PIECES + v] = leaves
            if v + far < PIECES:
                enters = (shift[v + far] >> bit) & 1
                comes[bit * PIECES + v] = enters
                shift[v] = jnp.where(enters > 0, shift[v + far], jnp.where(leaves > 0, 0, shift[v]))
            else:
                shift[v] = jnp.where(leaves > 0, 0, shift[v])

    def all_of(k, sem):
        pltpu.make_async_copy(R.at[k + 1, pl.ds(1, LON)], R.at[k + 1, pl.ds(1, LON)], sem).wait()

    verticals = [
        remote(R.at[1, pl.ds(1, LON)], R.at[LEV + 1, pl.ds(1, LON)], vs.at[0], vr.at[0], (c, up)),
        remote(R.at[LEV, pl.ds(1, LON)], R.at[0, pl.ds(1, LON)], vs.at[1], vr.at[1], (c, down)),
    ]

    def arrived(i, _):
        k = lax.select(i == 1, LEV - 1, lax.select(i == 0, 0, i - 1))
        all_of(k, fr.at[k])
        remote(R.at[k + 1, 1], R.at[k + 1, LON + 1], hs, hr.at[k], (left, s)).start()
        remote(R.at[k + 1, LON], R.at[k + 1, 0], hs, hr.at[k], (right, s)).start()

        @pl.when(i == 0)
        def _():
            verticals[0].start()

        @pl.when(i == 1)
        def _():
            verticals[1].start()

        @pl.when(i < LEV - AHEAD)
        def _():
            forward(i + AHEAD, 0)

        return 0

    edge = R.at[pl.ds(1, LEV), pl.ds(0, 2)]
    lax.fori_loop(0, 4, arrived, 0)

    tlane = lax.broadcasted_iota(jnp.int32, (TR, LAT), 1)

    def level(i, _):
        k = lax.select(i == LEV - 1, LEV - 1, lax.select(i == LEV - 2, 0, i + 1))

        both = R.at[k + 1, pl.ds(0, 2)]
        pltpu.make_async_copy(both, both, hr.at[k]).wait()

        @pl.when(i == LEV - 2)
        def _():
            verticals[1].wait_recv()

        @pl.when(i == LEV - 1)
        def _():
            verticals[0].wait_recv()

        def column(j, _):
            def row_of(n):
                return jnp.broadcast_to(coef[k, n, pl.ds(j, 1), :], (TR, LAT))

            center = R[k + 1, j + 1]
            moved = row_of(0) * center
            moved += row_of(1) * R[k + 1, j + 2]
            moved += row_of(2) * R[k + 1, j]
            moved += row_of(3) * jnp.where(tlane == LAT - 1, center, pltpu.roll(center, LAT - 1, 1))
            moved += row_of(4) * jnp.where(tlane == 0, center, pltpu.roll(center, 1, 1))
            moved += row_of(5) * R[k + 2, j + 1]
            moved += row_of(6) * R[k, j + 1]
            y = jnp.dot(lhs[...], stacked_halves(moved, saturating(moved)), preferred_element_type=F32)
            current = moved + y[:TR]
            base = current + y[TR:]
            y = jnp.dot(lhs[:TR, :], stacked_halves(current, saturating(current)), preferred_element_type=F32)
            wet_row = jnp.broadcast_to(wat_v[pl.ds(j, 1), :], (TR, LAT))
            reacted = jnp.where(wet_row > 0, base + y, moved)
            S[j] = reacted
            pig[k, pl.ds(j, 1), :] = reacted[0:1]
            return 0

        lax.fori_loop(0, LON, column, 0, unroll=2)

        @pl.when(i < LEV - 4)
        def _():
            arrived(i + 4, 0)

        return 0

    def give(i, _):
        k = lax.select(i == LEV - 1, LEV - 1, lax.select(i == LEV - 2, 0, i + 1))

        def pack(g, _):
            pieces = [
                along(S[v // 2, pl.ds(8 * g, 8), (v % 2) * HALF : (v % 2 + 1) * HALF], gather[v])
                for v in range(PIECES)
            ]
            for bit in range(BITS):
                far = 1 << bit
                for v in range(PIECES - far):
                    pieces[v] = jnp.where(comes[bit * PIECES + v] > 0, pieces[v + far], pieces[v])
            for v in range(2 * KEPT):
                C[k, v // 2, pl.ds(8 * g, 8), (v % 2) * HALF : (v % 2 + 1) * HALF] = pieces[v]
            return 0

        lax.fori_loop(0, TR // 8, pack, 0)

        for t in range(2):
            pltpu.make_async_copy(C.at[k, :, 2 * s + t, :], D.at[k, t, :, s, :], br.at[k]).start()

        def peer(r, _):
            d = (s + r) % SECS
            for t in range(2):
                remote(
                    C.at[k, :, 2 * d + t, :], D.at[k, t, :, s, :], bs.at[k], br.at[k], (c, d)
                ).start()
            return 0

        lax.fori_loop(1, SECS, peer, 0)

        return 0

    def both_of(i, _):
        level(i, 0)
        return give(i, 0)

    lax.fori_loop(0, LEV - 1, both_of, 0)
    level(LEV - 1, 0)

    total = jnp.zeros((LON, LAT), F32)
    for k in range(LEV):
        total += WATER_ABSORB + PIGMENT_ABSORB * saturating(pig[k])
    totals[s] = total

    def tell(r, _):
        remote(totals.at[s], totals.at[s], ts, tr_, (c, (s + r) % SECS)).start()
        return 0

    lax.fori_loop(1, SECS, tell, 0)
    give(LEV - 1, 0)
    sent = R.at[1, pl.ds(1, LON - 1)]

    def receive(i, _):
        k = lax.select(i == LEV - 1, LEV - 1, lax.select(i == LEV - 2, 0, i + 1))
        pltpu.make_async_copy(D.at[k], D.at[k], br.at[k]).wait()

        def unpack(n, _):
            t, half = n // 2, n % 2
            pieces = [
                D[k, t, v // 2, pl.ds(8 * half, 8), (v % 2) * HALF : (v % 2 + 1) * HALF]
                for v in range(2 * KEPT)
            ]
            pieces += [pieces[-1]] * (PIECES - 2 * KEPT)
            for bit in reversed(range(BITS)):
                far = 1 << bit
                for v in reversed(range(far, PIECES)):
                    pieces[v] = jnp.where(goes[bit * PIECES + v] > 0, pieces[v - far], pieces[v])
            pieces = [along(pieces[v], scatter[v]) for v in range(PIECES)]
            for group in range(2):
                for side in range(2):
                    lanes = slice(side * HALF, (side + 1) * HALF)
                    block = jnp.stack([pieces[2 * (8 * group + j) + side] for j in range(8)])
                    block = jnp.swapaxes(block, 0, 1)
                    here = wat_v[8 * group : 8 * group + 8, lanes] > 0
                    for d in range(8):
                        at = (t, LEV * (8 * half + d) + k, pl.ds(8 * group, 8), lanes)
                        sol_o[at] = jnp.where(here, block[d], sol_o[at])
            return 0

        lax.fori_loop(0, 4, unpack, 0)
        return 0

    original.wait()
    lax.fori_loop(0, LEV - 1, receive, 0)

    others = totals.at[pl.ds(0, SECS - 1)]
    pltpu.make_async_copy(others, others, tr_).wait()
    depth = jnp.zeros((LON, LAT), F32)
    for d in range(SECS):
        depth += totals[d] * jnp.where(d < s, 1.0, 0.0)
    light = CHLOROPHYLL_WARM * jnp.broadcast_to(lat_v[1:2, :], (LON, LAT)) * wet
    before = jnp.exp(-depth)
    for k in range(LEV):
        depth = depth + (WATER_ABSORB + PIGMENT_ABSORB * saturating(pig[k]))
        after = jnp.exp(-depth)
        thn_v[k] = thn_v[k] + light * (before - after)
        before = after
    outs.append(pltpu.make_async_copy(thn_v, th_o, osem.at[2]))
    outs[-1].start()

    receive(LEV - 1, 0)
    packed = goes.at[pl.ds(0, 2 * (SECS - 1) * KEPT * LAT // (8 * HALF))]

    def finish(k, _):
        pltpu.make_async_copy(sent, sent, fs.at[k]).wait()
        pltpu.make_async_copy(packed, packed, bs.at[k]).wait()
        return 0

    pltpu.make_async_copy(edge, edge, hs).wait()
    for copy in verticals:
        copy.wait_send()
    pltpu.make_async_copy(others, others, ts).wait()
    lax.fori_loop(0, LEV, finish, 0)
    for copy in outs:
        copy.wait()


def settle(*refs):
    given, made, sem = refs[:4], refs[4:8], refs[8]
    copies = [pltpu.make_async_copy(a, b, sem.at[i]) for i, (a, b) in enumerate(zip(given, made))]
    for copy in copies:
        copy.start()
    for copy in copies:
        copy.wait()


def on_device(thermal, flow, spreading, solute, lin, pre, ab, water):
    index = (np.arange(LAT, dtype=np.float64) + 0.5) * np.pi / LAT - np.pi / 2
    table = np.zeros((8, LAT), np.float32)
    table[0] = CORIOLIS * np.sin(index)
    table[1] = np.cos(index)
    hbm = pl.BlockSpec(memory_space=pltpu.HBM)
    dma = pltpu.SemaphoreType.DMA
    shapes = tuple(
        jax.ShapeDtypeStruct(a.shape, F32) for a in (thermal, flow, spreading, solute)
    )
    vmem = pl.BlockSpec(memory_space=pltpu.VMEM)
    given = (solute, flow, spreading, thermal, lin, pre, ab.reshape(1, TR), water, jnp.asarray(table))
    results = pl.pallas_call(
        kernel,
        out_shape=shapes,
        in_specs=[hbm] * 9,
        out_specs=(vmem,) * 4,
        scratch_shapes=[
            pltpu.VMEM((LEV + 2, LON + 2, TR, LAT), F32),
            pltpu.VMEM((LON, TR, LAT), F32),
            pltpu.VMEM((LEV, KEPT, TR, LAT), F32),
            pltpu.VMEM((LEV, 2, KEPT, SECS, LAT), F32),
            pltpu.VMEM((BITS * PIECES, 8, HALF), jnp.int32),
            pltpu.VMEM((BITS * PIECES, 8, HALF), jnp.int32),
            pltpu.VMEM((PIECES, 8, HALF), jnp.int32),
            pltpu.VMEM((PIECES, 8, HALF), jnp.int32),
            pltpu.VMEM((LEV, 7, LON, LAT), F32),
            pltpu.VMEM((2 * TR, LAT), BF16),
            pltpu.VMEM((2, LEV, LON, LAT), F32),
            pltpu.VMEM((LEV, LON, LAT), F32),
            pltpu.VMEM((LEV, LON, LAT), F32),
            pltpu.VMEM((TR, TR), F32),
            pltpu.VMEM((TR, TR), F32),
            pltpu.VMEM((1, TR), F32),
            pltpu.VMEM((LON, LAT), jnp.int32),
            pltpu.VMEM((8, LAT), F32),
            pltpu.VMEM((2, LON, LAT), F32),
            pltpu.VMEM((2, LON, LAT), F32),
            pltpu.VMEM((LON, LAT), F32),
            pltpu.VMEM((2, LEV, 8, LAT), F32),
            pltpu.VMEM((2, LEV, LON, LAT), F32),
            pltpu.VMEM((LEV, LON, LAT), F32),
            pltpu.VMEM((LEV, LON, LAT), F32),
            pltpu.VMEM((SECS, LON, LAT), F32),
            pltpu.VMEM((LEV, LON, LAT), F32),
            pltpu.VMEM((4, LON, LAT), jnp.int32),
            dma((8,)), dma((3,)), dma((5,)), dma((5,)),
            dma, dma((LEV,)), dma((LEV,)), dma((LEV,)), dma((2,)), dma((2,)), dma((LEV,)), dma((LEV,)),
            dma, dma, dma,
        ],
        compiler_params=pltpu.CompilerParams(
            collective_id=0, has_side_effects=True, vmem_limit_bytes=48 << 20
        ),
        name="ocean_step",
    )(*(pltpu.with_memory_space_constraint(a, pltpu.HBM) for a in given))
    return pl.pallas_call(
        settle,
        out_shape=shapes,
        in_specs=[vmem] * 4,
        out_specs=(hbm,) * 4,
        scratch_shapes=[dma((4,))],
        compiler_params=pltpu.CompilerParams(vmem_limit_bytes=16 << 20),
        name="settle",
    )(*results)


def solution(mesh):
    placed = (
        P("sec", "col", None),
        P(None, "sec", "col", None),
        P("sec", "col", None),
        P("sec", None, "col", None),
        P(),
        P(),
        P(),
        P("col", None),
    )
    return jax.shard_map(
        on_device,
        mesh=mesh,
        in_specs=placed,
        out_specs=placed[:1] + placed[1:4],
        check_vma=False,
    )
```

```python
import jax
import jax.numpy as jnp
import numpy as np
from jax import lax
from jax.experimental import pallas as pl
from jax.experimental.pallas import tpu as pltpu
from jax.sharding import PartitionSpec as P

CORIOLIS = 0.8
MIXING = 0.1
VERTICAL_MIX = 0.3
WATER_ABSORB = 0.02
PIGMENT_ABSORB = 0.06
CHLOROPHYLL_WARM = 10.0

SECS = 16
COLS = 8
LEV = 8
LON = 16
TR = 32
LAT = 256
AHEAD = 2
KEPT = 12
BITS = 5
HALF = 128
PIECES = LON * LAT // HALF
MESH = pl.DeviceIdType.MESH
F32 = jnp.float32
BF16 = jnp.bfloat16
HIGHEST = lax.Precision.HIGHEST


def saturating(value):
    return 1.0 - 1.0 / (1.0 + value * value)


def stacked_halves(top, bottom):
    both = jnp.concatenate([top, bottom], axis=0)
    high = both.astype(BF16)
    low = (both - high.astype(F32)).astype(BF16)
    return jnp.concatenate([high, low, high, low], axis=0)


def along(piece, index):
    return jnp.take_along_axis(piece, index, axis=1)


def kernel(
    x, flow, kap, th, lin, pre, ab, wat, lat,
    th_o, vel_o, kap_o, sol_o,
    R, S, C, D, comes, goes, gather, scatter, coef, lhs, flow_v, kap_v, th_v, lin_v, pre_v, ab_v, wat_v, lat_v,
    below_v, above_v, kabove_v, thh, vel_v, knext_v, pig, totals, thn_v, scr_v,
    lsem, osem, small_s, small_r, hs, hr, fs, fr, vs, vr, bs, br, ts, tr_, xs,
):
    c = lax.axis_index("col")
    s = lax.axis_index("sec")
    left, right = (c + COLS - 1) % COLS, (c + 1) % COLS
    up, down = (s + SECS - 1) % SECS, (s + 1) % SECS

    loads = [
        pltpu.make_async_copy(a, b, lsem.at[i])
        for i, (a, b) in enumerate(
            [(flow, flow_v), (kap, kap_v), (th, th_v), (lin, lin_v), (pre, pre_v), (ab, ab_v), (wat, wat_v), (lat, lat_v)]
        )
    ]
    for copy in loads:
        copy.start()

    barrier = pltpu.get_barrier_semaphore()

    def greet(r, _):
        pl.semaphore_signal(barrier, inc=1, device_id=(c, s ^ r), device_id_type=MESH)
        return 0

    lax.fori_loop(1, SECS, greet, 0)
    pl.semaphore_signal(barrier, inc=1, device_id=(left, s), device_id_type=MESH)
    pl.semaphore_signal(barrier, inc=1, device_id=(right, s), device_id_type=MESH)
    pl.semaphore_wait(barrier, SECS + 1)

    def remote(src, dst, send, recv, to):
        return pltpu.make_async_remote_copy(
            src_ref=src, dst_ref=dst, send_sem=send, recv_sem=recv, device_id=to, device_id_type=MESH
        )

    smalls = [
        remote(flow.at[:, 0], below_v, small_s.at[0], small_r.at[0], (c, up)),
        remote(flow.at[:, LEV - 1], above_v, small_s.at[1], small_r.at[1], (c, down)),
        remote(kap.at[LEV - 1], kabove_v, small_s.at[2], small_r.at[2], (c, down)),
        remote(th.at[:, 0, :], thh.at[1, :, 0, :], small_s.at[3], small_r.at[3], (left, s)),
        remote(th.at[:, LON - 1, :], thh.at[0, :, 0, :], small_s.at[4], small_r.at[4], (right, s)),
    ]
    for copy in smalls:
        copy.start()

    def forward(i, _):
        k = lax.select(i == 1, LEV - 1, lax.select(i == 0, 0, i - 1))
        for t in range(2):
            pltpu.make_async_copy(
                x.at[t, LEV * s + k], R.at[k + 1, pl.ds(1, LON), 2 * s + t, :], fr.at[k]
            ).start()

        def peer(r, _):
            d = (s + r) % SECS
            for t in range(2):
                remote(
                    x.at[t, LEV * d + k], R.at[k + 1, pl.ds(1, LON), 2 * s + t, :],
                    fs.at[k], fr.at[k], (c, d),
                ).start()
            return 0

        lax.fori_loop(1, SECS, peer, 0)
        return 0

    lax.fori_loop(0, AHEAD, forward, 0)

    original = pltpu.make_async_copy(x, sol_o, xs)
    original.start()

    def blank(end):
        def one(j, _):
            R[end, j + 1] = jnp.zeros((TR, LAT), F32)
            return 0

        lax.fori_loop(0, LON, one, 0)

    pl.when(s == 0)(lambda: blank(0))
    pl.when(s == SECS - 1)(lambda: blank(LEV + 1))

    for copy in loads:
        copy.wait()
    for copy in smalls:
        copy.wait()

    rot = jnp.broadcast_to(lat_v[0:1, :], (LON, LAT))
    inv = 1.0 + rot * rot
    wet = wat_v[...].astype(F32)
    row = lax.broadcasted_iota(jnp.int32, (LON, LAT), 0)
    lane = lax.broadcasted_iota(jnp.int32, (LON, LAT), 1)

    def turned(u, v):
        return (u + rot * v) / inv, (v - rot * u) / inv

    below_ok = jnp.where(s == SECS - 1, 0.0, 1.0)
    above_ok = jnp.where(s == 0, 0.0, 1.0)
    east_a, north_a = turned(above_v[0], above_v[1])
    east_b, north_b = turned(below_v[0], below_v[1])
    east, north = turned(flow_v[0, 0], flow_v[1, 0])
    shear = (east_a - east) ** 2 + (north_a - north) ** 2
    k_up = (0.5 * kabove_v[...] + 0.5 * shear / (1.0 + shear)) * (VERTICAL_MIX * above_ok) * wet
    for k in range(LEV):
        vel_v[0, k] = east
        vel_v[1, k] = north
        if k < LEV - 1:
            east_n, north_n = turned(flow_v[0, k + 1], flow_v[1, k + 1])
        else:
            east_n, north_n = east_b * below_ok, north_b * below_ok
        shear = (east - east_n) ** 2 + (north - north_n) ** 2
        knext = 0.5 * kap_v[k] + 0.5 * shear / (1.0 + shear)
        knext_v[k] = knext
        k_down = knext * VERTICAL_MIX * wet
        if k == LEV - 1:
            k_down = k_down * below_ok
        coef[k, 0] = (1.0 - 4.0 * MIXING * wet) - k_down - k_up
        coef[k, 1] = (MIXING - MIXING * east) * wet
        coef[k, 2] = (MIXING + MIXING * east) * wet
        coef[k, 3] = (MIXING - MIXING * north) * wet
        coef[k, 4] = (MIXING + MIXING * north) * wet
        coef[k, 5] = k_down
        coef[k, 6] = k_up
        f = th_v[k]
        f_e = jnp.where(row == LON - 1, jnp.broadcast_to(thh[1, k, 0:1, :], (LON, LAT)), pltpu.roll(f, LON - 1, 0))
        f_w = jnp.where(row == 0, jnp.broadcast_to(thh[0, k, 0:1, :], (LON, LAT)), pltpu.roll(f, 1, 0))
        f_n = jnp.where(lane == LAT - 1, f, pltpu.roll(f, LAT - 1, 1))
        f_s = jnp.where(lane == 0, f, pltpu.roll(f, 1, 1))
        thn_v[k] = (
            f + MIXING * (f_e + f_w + f_n + f_s - 4.0 * f)
            - MIXING * (east * (f_e - f_w) + north * (f_n - f_s))
        )
        east, north, k_up = east_n, north_n, k_down
    outs = [pltpu.make_async_copy(vel_v, vel_o, osem.at[0]), pltpu.make_async_copy(knext_v, kap_o, osem.at[1])]
    for copy in outs:
        copy.start()

    inner = jnp.dot(pre_v[...], lin_v[...], precision=HIGHEST, preferred_element_type=F32)
    scaled = pre_v[...] * ab_v[...]
    at = lax.broadcasted_iota(jnp.int32, (TR, LAT), 1)
    which = lax.broadcasted_iota(jnp.int32, (TR, LAT), 0)
    pick_m = (at % (2 * TR) == which).astype(F32)
    pick_s = (at % (2 * TR) == which + TR).astype(F32)
    first = jnp.dot(inner, pick_m, precision=HIGHEST, preferred_element_type=F32) - jnp.dot(
        scaled, pick_s, precision=HIGHEST, preferred_element_type=F32
    )
    second = -jnp.dot(pre_v[...], first, precision=HIGHEST, preferred_element_type=F32)
    for i, rows in enumerate((first, second)):
        high = rows.astype(BF16)
        low = rows - high.astype(F32)
        lhs[pl.ds(TR * i, TR), :] = jnp.where(at < 4 * TR, high.astype(F32), low).astype(BF16)

    lane8 = lax.broadcasted_iota(jnp.int32, (8, HALF), 1)
    wide = lax.broadcasted_iota(jnp.int32, (LAT, LAT), 0)
    wide_t = lax.broadcasted_iota(jnp.int32, (LAT, LAT), 1)
    same = wide // HALF == wide_t // HALF
    ahead_of = jnp.where(same & (wide < wide_t), 1.0, 0.0).astype(BF16)
    beside = jnp.where(same, 1.0, 0.0).astype(BF16)
    left_of = jnp.where(wide // HALF < wide_t // HALF, 1.0, 0.0).astype(BF16)
    row_t = lax.broadcasted_iota(jnp.int32, (LON, LON), 1)
    rows_before = jnp.where(lax.broadcasted_iota(jnp.int32, (LON, LON), 0) > row_t, 1.0, 0.0).astype(BF16)
    wet_b = wet.astype(BF16)
    rank = jnp.dot(wet_b, ahead_of, preferred_element_type=F32)
    before = jnp.dot(rows_before, wet_b, preferred_element_type=F32)
    before = jnp.dot(before.astype(BF16), jnp.ones((LAT, LAT), BF16), preferred_element_type=F32)
    before = before + jnp.dot(wet_b, left_of, preferred_element_type=F32)
    tables = [rank, before, jnp.dot(wet_b, beside, preferred_element_type=F32), wet]
    for i, table in enumerate(tables):
        scr_v[i] = table.astype(jnp.int32)

    def piece_of(i, v):
        part = scr_v[i, v // 2 : v // 2 + 1, (v % 2) * HALF : (v % 2 + 1) * HALF]
        return jnp.broadcast_to(part, (8, HALF))

    shift = []
    for v in range(PIECES):
        ranks, start, count, is_wet = (piece_of(i, v) for i in range(4))
        scatter[v] = (start + ranks) & (HALF - 1)
        lanes, moves = lane8, jnp.where(is_wet > 0, lane8 - ranks, 0)
        for bit in range(7):
            by = 1 << bit
            inside = lane8 < HALF - by
            next_m = jnp.where(inside, pltpu.roll(moves, HALF - by, 1), 0)
            enters = (next_m & by) > 0
            lanes = jnp.where(enters, pltpu.roll(lanes, HALF - by, 1), lanes)
            moves = jnp.where(enters, next_m, jnp.where((moves & by) > 0, 0, moves))
        turn = (lane8 - start) & (HALF - 1)
        gather[v] = along(lanes, turn)
        shift.append(jnp.where(turn < count, v - ((start + turn) >> 7), 0))
    for bit in range(BITS):
        far = 1 << bit
        for v in range(PIECES):
            leaves = (shift[v] >> bit) & 1
            goes[bit * PIECES + v] = leaves
            if v + far < PIECES:
                enters = (shift[v + far] >> bit) & 1
                comes[bit * PIECES + v] = enters
                shift[v] = jnp.where(enters > 0, shift[v + far], jnp.where(leaves > 0, 0, shift[v]))
            else:
                shift[v] = jnp.where(leaves > 0, 0, shift[v])

    def all_of(k, sem):
        pltpu.make_async_copy(R.at[k + 1, pl.ds(1, LON)], R.at[k + 1, pl.ds(1, LON)], sem).wait()

    verticals = [
        remote(R.at[1, pl.ds(1, LON)], R.at[LEV + 1, pl.ds(1, LON)], vs.at[0], vr.at[0], (c, up)),
        remote(R.at[LEV, pl.ds(1, LON)], R.at[0, pl.ds(1, LON)], vs.at[1], vr.at[1], (c, down)),
    ]

    def arrived(i, _):
        k = lax.select(i == 1, LEV - 1, lax.select(i == 0, 0, i - 1))
        all_of(k, fr.at[k])
        remote(R.at[k + 1, 1], R.at[k + 1, LON + 1], hs, hr.at[k], (left, s)).start()
        remote(R.at[k + 1, LON], R.at[k + 1, 0], hs, hr.at[k], (right, s)).start()

        @pl.when((i == 0) & (s > 0))
        def _():
            verticals[0].start()

        @pl.when((i == 1) & (s < SECS - 1))
        def _():
            verticals[1].start()

        @pl.when(i < LEV - AHEAD)
        def _():
            forward(i + AHEAD, 0)

        return 0

    edge = R.at[pl.ds(1, LEV), pl.ds(0, 2)]
    lax.fori_loop(0, 4, arrived, 0)

    tlane = lax.broadcasted_iota(jnp.int32, (TR, LAT), 1)

    def level(i, _):
        k = lax.select(i == LEV - 1, LEV - 1, lax.select(i == LEV - 2, 0, i + 1))

        both = R.at[k + 1, pl.ds(0, 2)]
        pltpu.make_async_copy(both, both, hr.at[k]).wait()

        @pl.when((i == LEV - 2) & (s > 0))
        def _():
            verticals[1].wait_recv()

        @pl.when((i == LEV - 1) & (s < SECS - 1))
        def _():
            verticals[0].wait_recv()

        def column(j, _):
            def row_of(n):
                return jnp.broadcast_to(coef[k, n, pl.ds(j, 1), :], (TR, LAT))

            center = R[k + 1, j + 1]
            moved = row_of(0) * center
            moved += row_of(1) * R[k + 1, j + 2]
            moved += row_of(2) * R[k + 1, j]
            moved += row_of(3) * jnp.where(tlane == LAT - 1, center, pltpu.roll(center, LAT - 1, 1))
            moved += row_of(4) * jnp.where(tlane == 0, center, pltpu.roll(center, 1, 1))
            moved += row_of(5) * R[k + 2, j + 1]
            moved += row_of(6) * R[k, j + 1]
            y = jnp.dot(lhs[...], stacked_halves(moved, saturating(moved)), preferred_element_type=F32)
            current = moved + y[:TR]
            base = current + y[TR:]
            y = jnp.dot(lhs[:TR, :], stacked_halves(current, saturating(current)), preferred_element_type=F32)
            wet_row = jnp.broadcast_to(wat_v[pl.ds(j, 1), :], (TR, LAT))
            reacted = jnp.where(wet_row > 0, base + y, moved)
            S[j] = reacted
            pig[k, pl.ds(j, 1), :] = reacted[0:1]
            return 0

        lax.fori_loop(0, LON, column, 0, unroll=2)

        @pl.when(i < LEV - 4)
        def _():
            arrived(i + 4, 0)

        return 0

    def give(i, _):
        k = lax.select(i == LEV - 1, LEV - 1, lax.select(i == LEV - 2, 0, i + 1))

        def pack(g, _):
            pieces = [
                along(S[v // 2, pl.ds(8 * g, 8), (v % 2) * HALF : (v % 2 + 1) * HALF], gather[v])
                for v in range(PIECES)
            ]
            for bit in range(BITS):
                far = 1 << bit
                for v in range(PIECES - far):
                    pieces[v] = jnp.where(comes[bit * PIECES + v] > 0, pieces[v + far], pieces[v])
            for v in range(2 * KEPT):
                C[k, v // 2, pl.ds(8 * g, 8), (v % 2) * HALF : (v % 2 + 1) * HALF] = pieces[v]
            return 0

        lax.fori_loop(0, TR // 8, pack, 0)

        for t in range(2):
            pltpu.make_async_copy(C.at[k, :, 2 * s + t, :], D.at[k, t, :, s, :], br.at[k]).start()

        def peer(r, _):
            d = (s + r) % SECS
            for t in range(2):
                remote(
                    C.at[k, :, 2 * d + t, :], D.at[k, t, :, s, :], bs.at[k], br.at[k], (c, d)
                ).start()
            return 0

        lax.fori_loop(1, SECS, peer, 0)

        return 0

    def both_of(i, _):
        level(i, 0)
        return give(i, 0)

    lax.fori_loop(0, LEV - 1, both_of, 0)
    level(LEV - 1, 0)

    total = jnp.zeros((LON, LAT), F32)
    for k in range(LEV):
        total += WATER_ABSORB + PIGMENT_ABSORB * saturating(pig[k])
    totals[s] = total

    def tell(r, _):
        remote(totals.at[s], totals.at[s], ts, tr_, (c, (s + r) % SECS)).start()
        return 0

    lax.fori_loop(1, SECS, tell, 0)
    give(LEV - 1, 0)
    sent = R.at[1, pl.ds(1, LON - 1)]

    def receive(i, _):
        k = lax.select(i == LEV - 1, LEV - 1, lax.select(i == LEV - 2, 0, i + 1))
        pltpu.make_async_copy(D.at[k], D.at[k], br.at[k]).wait()

        def unpack(n, _):
            t, half = n // 2, n % 2
            pieces = [
                D[k, t, v // 2, pl.ds(8 * half, 8), (v % 2) * HALF : (v % 2 + 1) * HALF]
                for v in range(2 * KEPT)
            ]
            pieces += [pieces[-1]] * (PIECES - 2 * KEPT)
            for bit in reversed(range(BITS)):
                far = 1 << bit
                for v in reversed(range(far, PIECES)):
                    pieces[v] = jnp.where(goes[bit * PIECES + v] > 0, pieces[v - far], pieces[v])
            pieces = [along(pieces[v], scatter[v]) for v in range(PIECES)]
            for group in range(2):
                for side in range(2):
                    lanes = slice(side * HALF, (side + 1) * HALF)
                    block = jnp.stack([pieces[2 * (8 * group + j) + side] for j in range(8)])
                    block = jnp.swapaxes(block, 0, 1)
                    here = wat_v[8 * group : 8 * group + 8, lanes] > 0
                    for d in range(8):
                        at = (t, LEV * (8 * half + d) + k, pl.ds(8 * group, 8), lanes)
                        sol_o[at] = jnp.where(here, block[d], sol_o[at])
            return 0

        lax.fori_loop(0, 4, unpack, 0)
        return 0

    original.wait()
    lax.fori_loop(0, LEV - 1, receive, 0)

    others = totals.at[pl.ds(0, SECS - 1)]
    pltpu.make_async_copy(others, others, tr_).wait()
    depth = jnp.zeros((LON, LAT), F32)
    for d in range(SECS):
        depth += totals[d] * jnp.where(d < s, 1.0, 0.0)
    light = CHLOROPHYLL_WARM * jnp.broadcast_to(lat_v[1:2, :], (LON, LAT)) * wet
    before = jnp.exp(-depth)
    for k in range(LEV):
        depth = depth + (WATER_ABSORB + PIGMENT_ABSORB * saturating(pig[k]))
        after = jnp.exp(-depth)
        thn_v[k] = thn_v[k] + light * (before - after)
        before = after
    outs.append(pltpu.make_async_copy(thn_v, th_o, osem.at[2]))
    outs[-1].start()

    receive(LEV - 1, 0)
    packed = goes.at[pl.ds(0, 2 * (SECS - 1) * KEPT * LAT // (8 * HALF))]

    def finish(k, _):
        pltpu.make_async_copy(sent, sent, fs.at[k]).wait()
        pltpu.make_async_copy(packed, packed, bs.at[k]).wait()
        return 0

    pltpu.make_async_copy(edge, edge, hs).wait()

    @pl.when(s > 0)
    def _():
        verticals[0].wait_send()

    @pl.when(s < SECS - 1)
    def _():
        verticals[1].wait_send()

    pltpu.make_async_copy(others, others, ts).wait()
    lax.fori_loop(0, LEV, finish, 0)
    for copy in outs:
        copy.wait()


def settle(*refs):
    given, made, sem = refs[:4], refs[4:8], refs[8]
    copies = [pltpu.make_async_copy(a, b, sem.at[i]) for i, (a, b) in enumerate(zip(given, made))]
    for copy in copies:
        copy.start()
    for copy in copies:
        copy.wait()


def on_device(thermal, flow, spreading, solute, lin, pre, ab, water):
    index = (np.arange(LAT, dtype=np.float64) + 0.5) * np.pi / LAT - np.pi / 2
    table = np.zeros((8, LAT), np.float32)
    table[0] = CORIOLIS * np.sin(index)
    table[1] = np.cos(index)
    hbm = pl.BlockSpec(memory_space=pltpu.HBM)
    dma = pltpu.SemaphoreType.DMA
    shapes = tuple(
        jax.ShapeDtypeStruct(a.shape, F32) for a in (thermal, flow, spreading, solute)
    )
    vmem = pl.BlockSpec(memory_space=pltpu.VMEM)
    given = (solute, flow, spreading, thermal, lin, pre, ab.reshape(1, TR), water, jnp.asarray(table))
    results = pl.pallas_call(
        kernel,
        out_shape=shapes,
        in_specs=[hbm] * 9,
        out_specs=(vmem,) * 4,
        scratch_shapes=[
            pltpu.VMEM((LEV + 2, LON + 2, TR, LAT), F32),
            pltpu.VMEM((LON, TR, LAT), F32),
            pltpu.VMEM((LEV, KEPT, TR, LAT), F32),
            pltpu.VMEM((LEV, 2, KEPT, SECS, LAT), F32),
            pltpu.VMEM((BITS * PIECES, 8, HALF), jnp.int32),
            pltpu.VMEM((BITS * PIECES, 8, HALF), jnp.int32),
            pltpu.VMEM((PIECES, 8, HALF), jnp.int32),
            pltpu.VMEM((PIECES, 8, HALF), jnp.int32),
            pltpu.VMEM((LEV, 7, LON, LAT), F32),
            pltpu.VMEM((2 * TR, LAT), BF16),
            pltpu.VMEM((2, LEV, LON, LAT), F32),
            pltpu.VMEM((LEV, LON, LAT), F32),
            pltpu.VMEM((LEV, LON, LAT), F32),
            pltpu.VMEM((TR, TR), F32),
            pltpu.VMEM((TR, TR), F32),
            pltpu.VMEM((1, TR), F32),
            pltpu.VMEM((LON, LAT), jnp.int32),
            pltpu.VMEM((8, LAT), F32),
            pltpu.VMEM((2, LON, LAT), F32),
            pltpu.VMEM((2, LON, LAT), F32),
            pltpu.VMEM((LON, LAT), F32),
            pltpu.VMEM((2, LEV, 8, LAT), F32),
            pltpu.VMEM((2, LEV, LON, LAT), F32),
            pltpu.VMEM((LEV, LON, LAT), F32),
            pltpu.VMEM((LEV, LON, LAT), F32),
            pltpu.VMEM((SECS, LON, LAT), F32),
            pltpu.VMEM((LEV, LON, LAT), F32),
            pltpu.VMEM((4, LON, LAT), jnp.int32),
            dma((8,)), dma((3,)), dma((5,)), dma((5,)),
            dma, dma((LEV,)), dma((LEV,)), dma((LEV,)), dma((2,)), dma((2,)), dma((LEV,)), dma((LEV,)),
            dma, dma, dma,
        ],
        compiler_params=pltpu.CompilerParams(
            collective_id=0, has_side_effects=True, vmem_limit_bytes=48 << 20
        ),
        name="ocean_step",
    )(*(pltpu.with_memory_space_constraint(a, pltpu.HBM) for a in given))
    return pl.pallas_call(
        settle,
        out_shape=shapes,
        in_specs=[vmem] * 4,
        out_specs=(hbm,) * 4,
        scratch_shapes=[dma((4,))],
        compiler_params=pltpu.CompilerParams(vmem_limit_bytes=16 << 20),
        name="settle",
    )(*results)


def solution(mesh):
    placed = (
        P("sec", "col", None),
        P(None, "sec", "col", None),
        P("sec", "col", None),
        P("sec", None, "col", None),
        P(),
        P(),
        P(),
        P("col", None),
    )
    return jax.shard_map(
        on_device,
        mesh=mesh,
        in_specs=placed,
        out_specs=placed[:1] + placed[1:4],
        check_vma=False,
    )
```

```python
import jax
import jax.numpy as jnp
import numpy as np
from jax import lax
from jax.experimental import pallas as pl
from jax.experimental.pallas import tpu as pltpu
from jax.sharding import PartitionSpec as P

CORIOLIS = 0.8
MIXING = 0.1
VERTICAL_MIX = 0.3
WATER_ABSORB = 0.02
PIGMENT_ABSORB = 0.06
CHLOROPHYLL_WARM = 10.0

SECS = 16
COLS = 8
LEV = 8
LON = 16
TR = 32
LAT = 256
AHEAD = 2
KEPT = 12
BITS = 5
HALF = 128
PIECES = LON * LAT // HALF
MESH = pl.DeviceIdType.MESH
F32 = jnp.float32
BF16 = jnp.bfloat16
HIGHEST = lax.Precision.HIGHEST


def saturating(value):
    return 1.0 - 1.0 / (1.0 + value * value)


def stacked_halves(top, bottom):
    both = jnp.concatenate([top, bottom], axis=0)
    high = both.astype(BF16)
    low = (both - high.astype(F32)).astype(BF16)
    return jnp.concatenate([high, low, high, low], axis=0)


def along(piece, index):
    return jnp.take_along_axis(piece, index, axis=1)


def kernel(
    x, flow, kap, th, lin, pre, ab, wat, lat,
    th_o, vel_o, kap_o, sol_o,
    R, S, C, D, comes, goes, gather, scatter, coef, lhs, flow_v, kap_v, th_v, lin_v, pre_v, ab_v, wat_v, lat_v,
    below_v, above_v, kabove_v, thh, vel_v, knext_v, pig, totals, thn_v, scr_v,
    lsem, osem, small_s, small_r, hs, hr, fs, fr, vs, vr, bs, br, ts, tr_, xs, VP, VQ,
):
    c = lax.axis_index("col")
    s = lax.axis_index("sec")
    left, right = (c + COLS - 1) % COLS, (c + 1) % COLS
    up, down = (s + SECS - 1) % SECS, (s + 1) % SECS

    loads = [
        pltpu.make_async_copy(a, b, lsem.at[i])
        for i, (a, b) in enumerate(
            [(flow, flow_v), (kap, kap_v), (th, th_v), (lin, lin_v), (pre, pre_v), (ab, ab_v), (wat, wat_v), (lat, lat_v)]
        )
    ]
    for copy in loads:
        copy.start()

    barrier = pltpu.get_barrier_semaphore()

    def greet(r, _):
        pl.semaphore_signal(barrier, inc=1, device_id=(c, s ^ r), device_id_type=MESH)
        return 0

    lax.fori_loop(1, SECS, greet, 0)
    pl.semaphore_signal(barrier, inc=1, device_id=(left, s), device_id_type=MESH)
    pl.semaphore_signal(barrier, inc=1, device_id=(right, s), device_id_type=MESH)
    pl.semaphore_wait(barrier, SECS + 1)

    def remote(src, dst, send, recv, to):
        return pltpu.make_async_remote_copy(
            src_ref=src, dst_ref=dst, send_sem=send, recv_sem=recv, device_id=to, device_id_type=MESH
        )

    smalls = [
        remote(flow.at[:, 0], below_v, small_s.at[0], small_r.at[0], (c, up)),
        remote(flow.at[:, LEV - 1], above_v, small_s.at[1], small_r.at[1], (c, down)),
        remote(kap.at[LEV - 1], kabove_v, small_s.at[2], small_r.at[2], (c, down)),
        remote(th.at[:, 0, :], thh.at[1, :, 0, :], small_s.at[3], small_r.at[3], (left, s)),
        remote(th.at[:, LON - 1, :], thh.at[0, :, 0, :], small_s.at[4], small_r.at[4], (right, s)),
    ]
    for copy in smalls:
        copy.start()

    def forward(i, _):
        k = lax.select(i == 1, LEV - 1, lax.select(i == 0, 0, i - 1))
        for t in range(2):
            pltpu.make_async_copy(
                x.at[t, LEV * s + k], R.at[k + 1, pl.ds(1, LON), 2 * s + t, :], fr.at[k]
            ).start()

        def peer(r, _):
            d = (s + r) % SECS
            for t in range(2):
                remote(
                    x.at[t, LEV * d + k], R.at[k + 1, pl.ds(1, LON), 2 * s + t, :],
                    fs.at[k], fr.at[k], (c, d),
                ).start()
            return 0

        lax.fori_loop(1, SECS, peer, 0)
        return 0

    lax.fori_loop(0, AHEAD, forward, 0)

    original = pltpu.make_async_copy(x, sol_o, xs)
    original.start()

    def blank(end):
        def one(j, _):
            R[end, j + 1] = jnp.zeros((TR, LAT), F32)
            return 0

        lax.fori_loop(0, LON, one, 0)

    pl.when(s == 0)(lambda: blank(0))
    pl.when(s == SECS - 1)(lambda: blank(LEV + 1))

    for copy in loads:
        copy.wait()
    for copy in smalls:
        copy.wait()

    rot = jnp.broadcast_to(lat_v[0:1, :], (LON, LAT))
    inv = 1.0 + rot * rot
    wet = wat_v[...].astype(F32)
    row = lax.broadcasted_iota(jnp.int32, (LON, LAT), 0)
    lane = lax.broadcasted_iota(jnp.int32, (LON, LAT), 1)

    def turned(u, v):
        return (u + rot * v) / inv, (v - rot * u) / inv

    below_ok = jnp.where(s == SECS - 1, 0.0, 1.0)
    above_ok = jnp.where(s == 0, 0.0, 1.0)
    east_a, north_a = turned(above_v[0], above_v[1])
    east_b, north_b = turned(below_v[0], below_v[1])
    east, north = turned(flow_v[0, 0], flow_v[1, 0])
    shear = (east_a - east) ** 2 + (north_a - north) ** 2
    k_up = (0.5 * kabove_v[...] + 0.5 * shear / (1.0 + shear)) * (VERTICAL_MIX * above_ok) * wet
    for k in range(LEV):
        vel_v[0, k] = east
        vel_v[1, k] = north
        if k < LEV - 1:
            east_n, north_n = turned(flow_v[0, k + 1], flow_v[1, k + 1])
        else:
            east_n, north_n = east_b * below_ok, north_b * below_ok
        shear = (east - east_n) ** 2 + (north - north_n) ** 2
        knext = 0.5 * kap_v[k] + 0.5 * shear / (1.0 + shear)
        knext_v[k] = knext
        k_down = knext * VERTICAL_MIX * wet
        if k == LEV - 1:
            k_down = k_down * below_ok
        coef[k, 0] = (1.0 - 4.0 * MIXING * wet) - k_down - k_up
        coef[k, 1] = (MIXING - MIXING * east) * wet
        coef[k, 2] = (MIXING + MIXING * east) * wet
        coef[k, 3] = (MIXING - MIXING * north) * wet
        coef[k, 4] = (MIXING + MIXING * north) * wet
        coef[k, 5] = k_down
        coef[k, 6] = k_up
        f = th_v[k]
        f_e = jnp.where(row == LON - 1, jnp.broadcast_to(thh[1, k, 0:1, :], (LON, LAT)), pltpu.roll(f, LON - 1, 0))
        f_w = jnp.where(row == 0, jnp.broadcast_to(thh[0, k, 0:1, :], (LON, LAT)), pltpu.roll(f, 1, 0))
        f_n = jnp.where(lane == LAT - 1, f, pltpu.roll(f, LAT - 1, 1))
        f_s = jnp.where(lane == 0, f, pltpu.roll(f, 1, 1))
        thn_v[k] = (
            f + MIXING * (f_e + f_w + f_n + f_s - 4.0 * f)
            - MIXING * (east * (f_e - f_w) + north * (f_n - f_s))
        )
        east, north, k_up = east_n, north_n, k_down
    outs = [pltpu.make_async_copy(vel_v, vel_o, osem.at[0]), pltpu.make_async_copy(knext_v, kap_o, osem.at[1])]
    for copy in outs:
        copy.start()

    inner = jnp.dot(pre_v[...], lin_v[...], precision=HIGHEST, preferred_element_type=F32)
    scaled = pre_v[...] * ab_v[...]
    at = lax.broadcasted_iota(jnp.int32, (TR, LAT), 1)
    which = lax.broadcasted_iota(jnp.int32, (TR, LAT), 0)
    pick_m = (at % (2 * TR) == which).astype(F32)
    pick_s = (at % (2 * TR) == which + TR).astype(F32)
    first = jnp.dot(inner, pick_m, precision=HIGHEST, preferred_element_type=F32) - jnp.dot(
        scaled, pick_s, precision=HIGHEST, preferred_element_type=F32
    )
    second = -jnp.dot(pre_v[...], first, precision=HIGHEST, preferred_element_type=F32)
    for i, rows in enumerate((first, second)):
        high = rows.astype(BF16)
        low = rows - high.astype(F32)
        lhs[pl.ds(TR * i, TR), :] = jnp.where(at < 4 * TR, high.astype(F32), low).astype(BF16)

    lane8 = lax.broadcasted_iota(jnp.int32, (8, HALF), 1)
    wide = lax.broadcasted_iota(jnp.int32, (LAT, LAT), 0)
    wide_t = lax.broadcasted_iota(jnp.int32, (LAT, LAT), 1)
    same = wide // HALF == wide_t // HALF
    ahead_of = jnp.where(same & (wide < wide_t), 1.0, 0.0).astype(BF16)
    beside = jnp.where(same, 1.0, 0.0).astype(BF16)
    left_of = jnp.where(wide // HALF < wide_t // HALF, 1.0, 0.0).astype(BF16)
    row_t = lax.broadcasted_iota(jnp.int32, (LON, LON), 1)
    rows_before = jnp.where(lax.broadcasted_iota(jnp.int32, (LON, LON), 0) > row_t, 1.0, 0.0).astype(BF16)
    wet_b = wet.astype(BF16)
    rank = jnp.dot(wet_b, ahead_of, preferred_element_type=F32)
    before = jnp.dot(rows_before, wet_b, preferred_element_type=F32)
    before = jnp.dot(before.astype(BF16), jnp.ones((LAT, LAT), BF16), preferred_element_type=F32)
    before = before + jnp.dot(wet_b, left_of, preferred_element_type=F32)
    tables = [rank, before, jnp.dot(wet_b, beside, preferred_element_type=F32), wet]
    for i, table in enumerate(tables):
        scr_v[i] = table.astype(jnp.int32)

    def piece_of(i, v):
        part = scr_v[i, v // 2 : v // 2 + 1, (v % 2) * HALF : (v % 2 + 1) * HALF]
        return jnp.broadcast_to(part, (8, HALF))

    shift = []
    for v in range(PIECES):
        ranks, start, count, is_wet = (piece_of(i, v) for i in range(4))
        scatter[v] = (start + ranks) & (HALF - 1)
        lanes, moves = lane8, jnp.where(is_wet > 0, lane8 - ranks, 0)
        for bit in range(7):
            by = 1 << bit
            inside = lane8 < HALF - by
            next_m = jnp.where(inside, pltpu.roll(moves, HALF - by, 1), 0)
            enters = (next_m & by) > 0
            lanes = jnp.where(enters, pltpu.roll(lanes, HALF - by, 1), lanes)
            moves = jnp.where(enters, next_m, jnp.where((moves & by) > 0, 0, moves))
        turn = (lane8 - start) & (HALF - 1)
        gather[v] = along(lanes, turn)
        shift.append(jnp.where(turn < count, v - ((start + turn) >> 7), 0))
    for bit in range(BITS):
        far = 1 << bit
        for v in range(PIECES):
            leaves = (shift[v] >> bit) & 1
            goes[bit * PIECES + v] = leaves
            if v + far < PIECES:
                enters = (shift[v + far] >> bit) & 1
                comes[bit * PIECES + v] = enters
                shift[v] = jnp.where(enters > 0, shift[v + far], jnp.where(leaves > 0, 0, shift[v]))
            else:
                shift[v] = jnp.where(leaves > 0, 0, shift[v])

    def all_of(k, sem):
        pltpu.make_async_copy(R.at[k + 1, pl.ds(1, LON)], R.at[k + 1, pl.ds(1, LON)], sem).wait()

    def places(g, first=0):
        return [
            (first + v // 2, pl.ds(pl.multiple_of(8 * g, 8), 8), slice((v % 2) * HALF, (v % 2 + 1) * HALF))
            for v in range(PIECES)
        ]

    def packed(pieces):
        pieces = [along(pieces[v], gather[v]) for v in range(PIECES)]
        for bit in range(BITS):
            far = 1 << bit
            for v in range(PIECES - far):
                pieces[v] = jnp.where(comes[bit * PIECES + v] > 0, pieces[v + far], pieces[v])
        return pieces

    def unpacked(pieces):
        pieces = pieces + [pieces[-1]] * (PIECES - 2 * KEPT)
        for bit in reversed(range(BITS)):
            far = 1 << bit
            for v in reversed(range(far, PIECES)):
                pieces[v] = jnp.where(goes[bit * PIECES + v] > 0, pieces[v - far], pieces[v])
        return [along(pieces[v], scatter[v]) for v in range(PIECES)]

    def pack_level(held, end):
        def one(g, _):
            pieces = packed([R[(held,) + at] for at in places(g, 1)])
            for at, piece in zip(places(g)[: 2 * KEPT], pieces):
                VP[(end,) + at] = piece
            return 0

        lax.fori_loop(0, TR // 8, one, 0)

    def unpack_level(end, held):
        def one(g, _):
            pieces = unpacked([VQ[(end,) + at] for at in places(g)[: 2 * KEPT]])
            for at, piece in zip(places(g, 1), pieces):
                R[(held,) + at] = piece
            return 0

        lax.fori_loop(0, TR // 8, one, 0)

    verticals = [
        remote(VP.at[0], VQ.at[1], vs.at[0], vr.at[0], (c, up)),
        remote(VP.at[1], VQ.at[0], vs.at[1], vr.at[1], (c, down)),
    ]

    def arrived(i, _):
        k = lax.select(i == 1, LEV - 1, lax.select(i == 0, 0, i - 1))
        all_of(k, fr.at[k])
        remote(R.at[k + 1, 1], R.at[k + 1, LON + 1], hs, hr.at[k], (left, s)).start()
        remote(R.at[k + 1, LON], R.at[k + 1, 0], hs, hr.at[k], (right, s)).start()

        @pl.when((i == 0) & (s > 0))
        def _():
            pack_level(1, 0)
            verticals[0].start()

        @pl.when((i == 1) & (s < SECS - 1))
        def _():
            pack_level(LEV, 1)
            verticals[1].start()

        @pl.when(i < LEV - AHEAD)
        def _():
            forward(i + AHEAD, 0)

        return 0

    edge = R.at[pl.ds(1, LEV), pl.ds(0, 2)]
    lax.fori_loop(0, 4, arrived, 0)

    tlane = lax.broadcasted_iota(jnp.int32, (TR, LAT), 1)

    def level(i, _):
        k = lax.select(i == LEV - 1, LEV - 1, lax.select(i == LEV - 2, 0, i + 1))

        both = R.at[k + 1, pl.ds(0, 2)]
        pltpu.make_async_copy(both, both, hr.at[k]).wait()

        @pl.when((i == LEV - 2) & (s > 0))
        def _():
            verticals[1].wait_recv()
            unpack_level(0, 0)

        @pl.when((i == LEV - 1) & (s < SECS - 1))
        def _():
            verticals[0].wait_recv()
            unpack_level(1, LEV + 1)

        def column(j, _):
            def row_of(n):
                return jnp.broadcast_to(coef[k, n, pl.ds(j, 1), :], (TR, LAT))

            center = R[k + 1, j + 1]
            moved = row_of(0) * center
            moved += row_of(1) * R[k + 1, j + 2]
            moved += row_of(2) * R[k + 1, j]
            moved += row_of(3) * jnp.where(tlane == LAT - 1, center, pltpu.roll(center, LAT - 1, 1))
            moved += row_of(4) * jnp.where(tlane == 0, center, pltpu.roll(center, 1, 1))
            moved += row_of(5) * R[k + 2, j + 1]
            moved += row_of(6) * R[k, j + 1]
            y = jnp.dot(lhs[...], stacked_halves(moved, saturating(moved)), preferred_element_type=F32)
            current = moved + y[:TR]
            base = current + y[TR:]
            y = jnp.dot(lhs[:TR, :], stacked_halves(current, saturating(current)), preferred_element_type=F32)
            wet_row = jnp.broadcast_to(wat_v[pl.ds(j, 1), :], (TR, LAT))
            reacted = jnp.where(wet_row > 0, base + y, moved)
            S[j] = reacted
            pig[k, pl.ds(j, 1), :] = reacted[0:1]
            return 0

        lax.fori_loop(0, LON, column, 0, unroll=2)

        @pl.when(i < LEV - 4)
        def _():
            arrived(i + 4, 0)

        return 0

    def give(i, _):
        k = lax.select(i == LEV - 1, LEV - 1, lax.select(i == LEV - 2, 0, i + 1))

        def pack(g, _):
            pieces = packed([S[at] for at in places(g)])
            for v in range(2 * KEPT):
                C[k, v // 2, pl.ds(8 * g, 8), (v % 2) * HALF : (v % 2 + 1) * HALF] = pieces[v]
            return 0

        lax.fori_loop(0, TR // 8, pack, 0)

        for t in range(2):
            pltpu.make_async_copy(C.at[k, :, 2 * s + t, :], D.at[k, t, :, s, :], br.at[k]).start()

        def peer(r, _):
            d = (s + r) % SECS
            for t in range(2):
                remote(
                    C.at[k, :, 2 * d + t, :], D.at[k, t, :, s, :], bs.at[k], br.at[k], (c, d)
                ).start()
            return 0

        lax.fori_loop(1, SECS, peer, 0)

        return 0

    def both_of(i, _):
        level(i, 0)
        return give(i, 0)

    lax.fori_loop(0, LEV - 1, both_of, 0)
    level(LEV - 1, 0)

    total = jnp.zeros((LON, LAT), F32)
    for k in range(LEV):
        total += WATER_ABSORB + PIGMENT_ABSORB * saturating(pig[k])
    totals[s] = total

    def tell(r, _):
        remote(totals.at[s], totals.at[s], ts, tr_, (c, (s + r) % SECS)).start()
        return 0

    lax.fori_loop(1, SECS, tell, 0)
    give(LEV - 1, 0)
    sent = R.at[1, pl.ds(1, LON - 1)]

    def receive(i, _):
        k = lax.select(i == LEV - 1, LEV - 1, lax.select(i == LEV - 2, 0, i + 1))
        pltpu.make_async_copy(D.at[k], D.at[k], br.at[k]).wait()

        def unpack(n, _):
            t, half = n // 2, n % 2
            pieces = [
                D[k, t, v // 2, pl.ds(8 * half, 8), (v % 2) * HALF : (v % 2 + 1) * HALF]
                for v in range(2 * KEPT)
            ]
            pieces = unpacked(pieces)
            for group in range(2):
                for side in range(2):
                    lanes = slice(side * HALF, (side + 1) * HALF)
                    block = jnp.stack([pieces[2 * (8 * group + j) + side] for j in range(8)])
                    block = jnp.swapaxes(block, 0, 1)
                    here = wat_v[8 * group : 8 * group + 8, lanes] > 0
                    for d in range(8):
                        at = (t, LEV * (8 * half + d) + k, pl.ds(8 * group, 8), lanes)
                        sol_o[at] = jnp.where(here, block[d], sol_o[at])
            return 0

        lax.fori_loop(0, 4, unpack, 0)
        return 0

    original.wait()
    lax.fori_loop(0, LEV - 1, receive, 0)

    others = totals.at[pl.ds(0, SECS - 1)]
    pltpu.make_async_copy(others, others, tr_).wait()
    depth = jnp.zeros((LON, LAT), F32)
    for d in range(SECS):
        depth += totals[d] * jnp.where(d < s, 1.0, 0.0)
    light = CHLOROPHYLL_WARM * jnp.broadcast_to(lat_v[1:2, :], (LON, LAT)) * wet
    before = jnp.exp(-depth)
    for k in range(LEV):
        depth = depth + (WATER_ABSORB + PIGMENT_ABSORB * saturating(pig[k]))
        after = jnp.exp(-depth)
        thn_v[k] = thn_v[k] + light * (before - after)
        before = after
    outs.append(pltpu.make_async_copy(thn_v, th_o, osem.at[2]))
    outs[-1].start()

    receive(LEV - 1, 0)
    packed = goes.at[pl.ds(0, 2 * (SECS - 1) * KEPT * LAT // (8 * HALF))]

    def finish(k, _):
        pltpu.make_async_copy(sent, sent, fs.at[k]).wait()
        pltpu.make_async_copy(packed, packed, bs.at[k]).wait()
        return 0

    pltpu.make_async_copy(edge, edge, hs).wait()

    @pl.when(s > 0)
    def _():
        verticals[0].wait_send()

    @pl.when(s < SECS - 1)
    def _():
        verticals[1].wait_send()

    pltpu.make_async_copy(others, others, ts).wait()
    lax.fori_loop(0, LEV, finish, 0)
    for copy in outs:
        copy.wait()


def settle(*refs):
    given, made, sem = refs[:4], refs[4:8], refs[8]
    copies = [pltpu.make_async_copy(a, b, sem.at[i]) for i, (a, b) in enumerate(zip(given, made))]
    for copy in copies:
        copy.start()
    for copy in copies:
        copy.wait()


def on_device(thermal, flow, spreading, solute, lin, pre, ab, water):
    index = (np.arange(LAT, dtype=np.float64) + 0.5) * np.pi / LAT - np.pi / 2
    table = np.zeros((8, LAT), np.float32)
    table[0] = CORIOLIS * np.sin(index)
    table[1] = np.cos(index)
    hbm = pl.BlockSpec(memory_space=pltpu.HBM)
    dma = pltpu.SemaphoreType.DMA
    shapes = tuple(
        jax.ShapeDtypeStruct(a.shape, F32) for a in (thermal, flow, spreading, solute)
    )
    vmem = pl.BlockSpec(memory_space=pltpu.VMEM)
    given = (solute, flow, spreading, thermal, lin, pre, ab.reshape(1, TR), water, jnp.asarray(table))
    results = pl.pallas_call(
        kernel,
        out_shape=shapes,
        in_specs=[hbm] * 9,
        out_specs=(vmem,) * 4,
        scratch_shapes=[
            pltpu.VMEM((LEV + 2, LON + 2, TR, LAT), F32),
            pltpu.VMEM((LON, TR, LAT), F32),
            pltpu.VMEM((LEV, KEPT, TR, LAT), F32),
            pltpu.VMEM((LEV, 2, KEPT, SECS, LAT), F32),
            pltpu.VMEM((BITS * PIECES, 8, HALF), jnp.int32),
            pltpu.VMEM((BITS * PIECES, 8, HALF), jnp.int32),
            pltpu.VMEM((PIECES, 8, HALF), jnp.int32),
            pltpu.VMEM((PIECES, 8, HALF), jnp.int32),
            pltpu.VMEM((LEV, 7, LON, LAT), F32),
            pltpu.VMEM((2 * TR, LAT), BF16),
            pltpu.VMEM((2, LEV, LON, LAT), F32),
            pltpu.VMEM((LEV, LON, LAT), F32),
            pltpu.VMEM((LEV, LON, LAT), F32),
            pltpu.VMEM((TR, TR), F32),
            pltpu.VMEM((TR, TR), F32),
            pltpu.VMEM((1, TR), F32),
            pltpu.VMEM((LON, LAT), jnp.int32),
            pltpu.VMEM((8, LAT), F32),
            pltpu.VMEM((2, LON, LAT), F32),
            pltpu.VMEM((2, LON, LAT), F32),
            pltpu.VMEM((LON, LAT), F32),
            pltpu.VMEM((2, LEV, 8, LAT), F32),
            pltpu.VMEM((2, LEV, LON, LAT), F32),
            pltpu.VMEM((LEV, LON, LAT), F32),
            pltpu.VMEM((LEV, LON, LAT), F32),
            pltpu.VMEM((SECS, LON, LAT), F32),
            pltpu.VMEM((LEV, LON, LAT), F32),
            pltpu.VMEM((4, LON, LAT), jnp.int32),
            dma((8,)), dma((3,)), dma((5,)), dma((5,)),
            dma, dma((LEV,)), dma((LEV,)), dma((LEV,)), dma((2,)), dma((2,)), dma((LEV,)), dma((LEV,)),
            dma, dma, dma,
            pltpu.VMEM((2, KEPT, TR, LAT), F32),
            pltpu.VMEM((2, KEPT, TR, LAT), F32),
        ],
        compiler_params=pltpu.CompilerParams(
            collective_id=0, has_side_effects=True, vmem_limit_bytes=48 << 20
        ),
        name="ocean_step",
    )(*(pltpu.with_memory_space_constraint(a, pltpu.HBM) for a in given))
    return pl.pallas_call(
        settle,
        out_shape=shapes,
        in_specs=[vmem] * 4,
        out_specs=(hbm,) * 4,
        scratch_shapes=[dma((4,))],
        compiler_params=pltpu.CompilerParams(vmem_limit_bytes=16 << 20),
        name="settle",
    )(*results)


def solution(mesh):
    placed = (
        P("sec", "col", None),
        P(None, "sec", "col", None),
        P("sec", "col", None),
        P("sec", None, "col", None),
        P(),
        P(),
        P(),
        P("col", None),
    )
    return jax.shard_map(
        on_device,
        mesh=mesh,
        in_specs=placed,
        out_specs=placed[:1] + placed[1:4],
        check_vma=False,
    )
```

```python
import jax
import jax.numpy as jnp
import numpy as np
from jax import lax
from jax.experimental import pallas as pl
from jax.experimental.pallas import tpu as pltpu
from jax.sharding import PartitionSpec as P

CORIOLIS = 0.8
MIXING = 0.1
VERTICAL_MIX = 0.3
WATER_ABSORB = 0.02
PIGMENT_ABSORB = 0.06
CHLOROPHYLL_WARM = 10.0

SECS = 16
COLS = 8
LEV = 8
LON = 16
TR = 32
LAT = 256
AHEAD = 2
KEPT = 12
BITS = 5
HALF = 128
PIECES = LON * LAT // HALF
MESH = pl.DeviceIdType.MESH
F32 = jnp.float32
BF16 = jnp.bfloat16
HIGHEST = lax.Precision.HIGHEST


def saturating(value):
    return 1.0 - 1.0 / (1.0 + value * value)


def stacked_halves(top, bottom):
    both = jnp.concatenate([top, bottom], axis=0)
    high = both.astype(BF16)
    low = (both - high.astype(F32)).astype(BF16)
    return jnp.concatenate([high, low, high, low], axis=0)


def along(piece, index):
    return jnp.take_along_axis(piece, index, axis=1)


def kernel(
    x, flow, kap, th, lin, pre, ab, wat, lat,
    th_o, vel_o, kap_o, sol_o,
    R, S, C, D, comes, goes, gather, scatter, coef, lhs, flow_v, kap_v, th_v, lin_v, pre_v, ab_v, wat_v, lat_v,
    below_v, above_v, kabove_v, thh, vel_v, knext_v, pig, totals, thn_v, scr_v,
    lsem, osem, small_s, small_r, hs, hr, fs, fr, vs, vr, bs, br, ts, tr_, xs, VP, VQ,
):
    c = lax.axis_index("col")
    s = lax.axis_index("sec")
    left, right = (c + COLS - 1) % COLS, (c + 1) % COLS
    up, down = (s + SECS - 1) % SECS, (s + 1) % SECS

    loads = [
        pltpu.make_async_copy(a, b, lsem.at[i])
        for i, (a, b) in enumerate(
            [(flow, flow_v), (kap, kap_v), (th, th_v), (lin, lin_v), (pre, pre_v), (ab, ab_v), (wat, wat_v), (lat, lat_v)]
        )
    ]
    barrier = pltpu.get_barrier_semaphore()

    def greet(r, _):
        pl.semaphore_signal(barrier, inc=1, device_id=(c, s ^ r), device_id_type=MESH)
        return 0

    lax.fori_loop(1, SECS, greet, 0)
    pl.semaphore_signal(barrier, inc=1, device_id=(left, s), device_id_type=MESH)
    pl.semaphore_signal(barrier, inc=1, device_id=(right, s), device_id_type=MESH)
    for copy in loads:
        copy.start()
    pl.semaphore_wait(barrier, SECS + 1)

    def remote(src, dst, send, recv, to):
        return pltpu.make_async_remote_copy(
            src_ref=src, dst_ref=dst, send_sem=send, recv_sem=recv, device_id=to, device_id_type=MESH
        )

    smalls = [
        remote(flow.at[:, 0], below_v, small_s.at[0], small_r.at[0], (c, up)),
        remote(flow.at[:, LEV - 1], above_v, small_s.at[1], small_r.at[1], (c, down)),
        remote(kap.at[LEV - 1], kabove_v, small_s.at[2], small_r.at[2], (c, down)),
        remote(th.at[:, 0, :], thh.at[1, :, 0, :], small_s.at[3], small_r.at[3], (left, s)),
        remote(th.at[:, LON - 1, :], thh.at[0, :, 0, :], small_s.at[4], small_r.at[4], (right, s)),
    ]
    for copy in smalls:
        copy.start()

    def forward(i, _):
        k = lax.select(i == 1, LEV - 1, lax.select(i == 0, 0, i - 1))
        for t in range(2):
            pltpu.make_async_copy(
                x.at[t, LEV * s + k], R.at[k + 1, pl.ds(1, LON), 2 * s + t, :], fr.at[k]
            ).start()

        def peer(r, _):
            d = (s + r) % SECS
            for t in range(2):
                remote(
                    x.at[t, LEV * d + k], R.at[k + 1, pl.ds(1, LON), 2 * s + t, :],
                    fs.at[k], fr.at[k], (c, d),
                ).start()
            return 0

        lax.fori_loop(1, SECS, peer, 0)
        return 0

    lax.fori_loop(0, AHEAD, forward, 0)

    original = pltpu.make_async_copy(x, sol_o, xs)
    original.start()

    def blank(end):
        def one(j, _):
            R[end, j + 1] = jnp.zeros((TR, LAT), F32)
            return 0

        lax.fori_loop(0, LON, one, 0)

    pl.when(s == 0)(lambda: blank(0))
    pl.when(s == SECS - 1)(lambda: blank(LEV + 1))

    for copy in loads:
        copy.wait()
    for copy in smalls:
        copy.wait()

    rot = jnp.broadcast_to(lat_v[0:1, :], (LON, LAT))
    inv = 1.0 + rot * rot
    wet = wat_v[...].astype(F32)
    row = lax.broadcasted_iota(jnp.int32, (LON, LAT), 0)
    lane = lax.broadcasted_iota(jnp.int32, (LON, LAT), 1)

    def turned(u, v):
        return (u + rot * v) / inv, (v - rot * u) / inv

    below_ok = jnp.where(s == SECS - 1, 0.0, 1.0)
    above_ok = jnp.where(s == 0, 0.0, 1.0)
    east_a, north_a = turned(above_v[0], above_v[1])
    east_b, north_b = turned(below_v[0], below_v[1])
    east, north = turned(flow_v[0, 0], flow_v[1, 0])
    shear = (east_a - east) ** 2 + (north_a - north) ** 2
    k_up = (0.5 * kabove_v[...] + 0.5 * shear / (1.0 + shear)) * (VERTICAL_MIX * above_ok) * wet
    for k in range(LEV):
        vel_v[0, k] = east
        vel_v[1, k] = north
        if k < LEV - 1:
            east_n, north_n = turned(flow_v[0, k + 1], flow_v[1, k + 1])
        else:
            east_n, north_n = east_b * below_ok, north_b * below_ok
        shear = (east - east_n) ** 2 + (north - north_n) ** 2
        knext = 0.5 * kap_v[k] + 0.5 * shear / (1.0 + shear)
        knext_v[k] = knext
        k_down = knext * VERTICAL_MIX * wet
        if k == LEV - 1:
            k_down = k_down * below_ok
        coef[k, 0] = (1.0 - 4.0 * MIXING * wet) - k_down - k_up
        coef[k, 1] = (MIXING - MIXING * east) * wet
        coef[k, 2] = (MIXING + MIXING * east) * wet
        coef[k, 3] = (MIXING - MIXING * north) * wet
        coef[k, 4] = (MIXING + MIXING * north) * wet
        coef[k, 5] = k_down
        coef[k, 6] = k_up
        f = th_v[k]
        f_e = jnp.where(row == LON - 1, jnp.broadcast_to(thh[1, k, 0:1, :], (LON, LAT)), pltpu.roll(f, LON - 1, 0))
        f_w = jnp.where(row == 0, jnp.broadcast_to(thh[0, k, 0:1, :], (LON, LAT)), pltpu.roll(f, 1, 0))
        f_n = jnp.where(lane == LAT - 1, f, pltpu.roll(f, LAT - 1, 1))
        f_s = jnp.where(lane == 0, f, pltpu.roll(f, 1, 1))
        thn_v[k] = (
            f + MIXING * (f_e + f_w + f_n + f_s - 4.0 * f)
            - MIXING * (east * (f_e - f_w) + north * (f_n - f_s))
        )
        east, north, k_up = east_n, north_n, k_down
    outs = [pltpu.make_async_copy(vel_v, vel_o, osem.at[0]), pltpu.make_async_copy(knext_v, kap_o, osem.at[1])]
    for copy in outs:
        copy.start()

    inner = jnp.dot(pre_v[...], lin_v[...], precision=HIGHEST, preferred_element_type=F32)
    scaled = pre_v[...] * ab_v[...]
    at = lax.broadcasted_iota(jnp.int32, (TR, LAT), 1)
    which = lax.broadcasted_iota(jnp.int32, (TR, LAT), 0)
    pick_m = (at % (2 * TR) == which).astype(F32)
    pick_s = (at % (2 * TR) == which + TR).astype(F32)
    first = jnp.dot(inner, pick_m, precision=HIGHEST, preferred_element_type=F32) - jnp.dot(
        scaled, pick_s, precision=HIGHEST, preferred_element_type=F32
    )
    second = -jnp.dot(pre_v[...], first, precision=HIGHEST, preferred_element_type=F32)
    for i, rows in enumerate((first, second)):
        high = rows.astype(BF16)
        low = rows - high.astype(F32)
        lhs[pl.ds(TR * i, TR), :] = jnp.where(at < 4 * TR, high.astype(F32), low).astype(BF16)

    lane8 = lax.broadcasted_iota(jnp.int32, (8, HALF), 1)
    wide = lax.broadcasted_iota(jnp.int32, (LAT, LAT), 0)
    wide_t = lax.broadcasted_iota(jnp.int32, (LAT, LAT), 1)
    same = wide // HALF == wide_t // HALF
    ahead_of = jnp.where(same & (wide < wide_t), 1.0, 0.0).astype(BF16)
    beside = jnp.where(same, 1.0, 0.0).astype(BF16)
    left_of = jnp.where(wide // HALF < wide_t // HALF, 1.0, 0.0).astype(BF16)
    row_t = lax.broadcasted_iota(jnp.int32, (LON, LON), 1)
    rows_before = jnp.where(lax.broadcasted_iota(jnp.int32, (LON, LON), 0) > row_t, 1.0, 0.0).astype(BF16)
    wet_b = wet.astype(BF16)
    rank = jnp.dot(wet_b, ahead_of, preferred_element_type=F32)
    before = jnp.dot(rows_before, wet_b, preferred_element_type=F32)
    before = jnp.dot(before.astype(BF16), jnp.ones((LAT, LAT), BF16), preferred_element_type=F32)
    before = before + jnp.dot(wet_b, left_of, preferred_element_type=F32)
    tables = [rank, before, jnp.dot(wet_b, beside, preferred_element_type=F32), wet]
    for i, table in enumerate(tables):
        scr_v[i] = table.astype(jnp.int32)

    def piece_of(i, v):
        part = scr_v[i, v // 2 : v // 2 + 1, (v % 2) * HALF : (v % 2 + 1) * HALF]
        return jnp.broadcast_to(part, (8, HALF))

    shift = []
    for v in range(PIECES):
        ranks, start, count, is_wet = (piece_of(i, v) for i in range(4))
        scatter[v] = (start + ranks) & (HALF - 1)
        lanes, moves = lane8, jnp.where(is_wet > 0, lane8 - ranks, 0)
        for bit in range(7):
            by = 1 << bit
            inside = lane8 < HALF - by
            next_m = jnp.where(inside, pltpu.roll(moves, HALF - by, 1), 0)
            enters = (next_m & by) > 0
            lanes = jnp.where(enters, pltpu.roll(lanes, HALF - by, 1), lanes)
            moves = jnp.where(enters, next_m, jnp.where((moves & by) > 0, 0, moves))
        turn = (lane8 - start) & (HALF - 1)
        gather[v] = along(lanes, turn)
        shift.append(jnp.where(turn < count, v - ((start + turn) >> 7), 0))
    for bit in range(BITS):
        far = 1 << bit
        for v in range(PIECES):
            leaves = (shift[v] >> bit) & 1
            goes[bit * PIECES + v] = leaves
            if v + far < PIECES:
                enters = (shift[v + far] >> bit) & 1
                comes[bit * PIECES + v] = enters
                shift[v] = jnp.where(enters > 0, shift[v + far], jnp.where(leaves > 0, 0, shift[v]))
            else:
                shift[v] = jnp.where(leaves > 0, 0, shift[v])

    def all_of(k, sem):
        pltpu.make_async_copy(R.at[k + 1, pl.ds(1, LON)], R.at[k + 1, pl.ds(1, LON)], sem).wait()

    def places(g, first=0):
        return [
            (first + v // 2, pl.ds(pl.multiple_of(8 * g, 8), 8), slice((v % 2) * HALF, (v % 2 + 1) * HALF))
            for v in range(PIECES)
        ]

    def packed(pieces):
        pieces = [along(pieces[v], gather[v]) for v in range(PIECES)]
        for bit in range(BITS):
            far = 1 << bit
            for v in range(PIECES - far):
                pieces[v] = jnp.where(comes[bit * PIECES + v] > 0, pieces[v + far], pieces[v])
        return pieces

    def unpacked(pieces):
        pieces = pieces + [pieces[-1]] * (PIECES - 2 * KEPT)
        for bit in reversed(range(BITS)):
            far = 1 << bit
            for v in reversed(range(far, PIECES)):
                pieces[v] = jnp.where(goes[bit * PIECES + v] > 0, pieces[v - far], pieces[v])
        return [along(pieces[v], scatter[v]) for v in range(PIECES)]

    def pack_level(held, end):
        def one(g, _):
            pieces = packed([R[(held,) + at] for at in places(g, 1)])
            for at, piece in zip(places(g)[: 2 * KEPT], pieces):
                VP[(end,) + at] = piece
            return 0

        lax.fori_loop(0, TR // 8, one, 0)

    def unpack_level(end, held):
        def one(g, _):
            pieces = unpacked([VQ[(end,) + at] for at in places(g)[: 2 * KEPT]])
            for at, piece in zip(places(g, 1), pieces):
                R[(held,) + at] = piece
            return 0

        lax.fori_loop(0, TR // 8, one, 0)

    verticals = [
        remote(VP.at[0], VQ.at[1], vs.at[0], vr.at[0], (c, up)),
        remote(VP.at[1], VQ.at[0], vs.at[1], vr.at[1], (c, down)),
    ]

    def arrived(i, _):
        k = lax.select(i == 1, LEV - 1, lax.select(i == 0, 0, i - 1))
        all_of(k, fr.at[k])
        remote(R.at[k + 1, 1], R.at[k + 1, LON + 1], hs, hr.at[k], (left, s)).start()
        remote(R.at[k + 1, LON], R.at[k + 1, 0], hs, hr.at[k], (right, s)).start()

        @pl.when((i == 0) & (s > 0))
        def _():
            pack_level(1, 0)
            verticals[0].start()

        @pl.when((i == 1) & (s < SECS - 1))
        def _():
            pack_level(LEV, 1)
            verticals[1].start()

        @pl.when(i < LEV - AHEAD)
        def _():
            forward(i + AHEAD, 0)

        return 0

    edge = R.at[pl.ds(1, LEV), pl.ds(0, 2)]
    lax.fori_loop(0, 4, arrived, 0)

    tlane = lax.broadcasted_iota(jnp.int32, (TR, LAT), 1)

    def level(i, _):
        k = lax.select(i == LEV - 1, LEV - 1, lax.select(i == LEV - 2, 0, i + 1))

        both = R.at[k + 1, pl.ds(0, 2)]
        pltpu.make_async_copy(both, both, hr.at[k]).wait()

        @pl.when((i == LEV - 2) & (s > 0))
        def _():
            verticals[1].wait_recv()
            unpack_level(0, 0)

        @pl.when((i == LEV - 1) & (s < SECS - 1))
        def _():
            verticals[0].wait_recv()
            unpack_level(1, LEV + 1)

        def column(j, _):
            def row_of(n):
                return jnp.broadcast_to(coef[k, n, pl.ds(j, 1), :], (TR, LAT))

            center = R[k + 1, j + 1]
            moved = row_of(0) * center
            moved += row_of(1) * R[k + 1, j + 2]
            moved += row_of(2) * R[k + 1, j]
            moved += row_of(3) * jnp.where(tlane == LAT - 1, center, pltpu.roll(center, LAT - 1, 1))
            moved += row_of(4) * jnp.where(tlane == 0, center, pltpu.roll(center, 1, 1))
            moved += row_of(5) * R[k + 2, j + 1]
            moved += row_of(6) * R[k, j + 1]
            y = jnp.dot(lhs[...], stacked_halves(moved, saturating(moved)), preferred_element_type=F32)
            current = moved + y[:TR]
            base = current + y[TR:]
            y = jnp.dot(lhs[:TR, :], stacked_halves(current, saturating(current)), preferred_element_type=F32)
            wet_row = jnp.broadcast_to(wat_v[pl.ds(j, 1), :], (TR, LAT))
            reacted = jnp.where(wet_row > 0, base + y, moved)
            S[j] = reacted
            pig[k, pl.ds(j, 1), :] = reacted[0:1]
            return 0

        lax.fori_loop(0, LON, column, 0, unroll=2)

        @pl.when(i < LEV - 4)
        def _():
            arrived(i + 4, 0)

        return 0

    def give(i, _):
        k = lax.select(i == LEV - 1, LEV - 1, lax.select(i == LEV - 2, 0, i + 1))

        def pack(g, _):
            pieces = packed([S[at] for at in places(g)])
            for v in range(2 * KEPT):
                C[k, v // 2, pl.ds(8 * g, 8), (v % 2) * HALF : (v % 2 + 1) * HALF] = pieces[v]
            return 0

        lax.fori_loop(0, TR // 8, pack, 0)

        for t in range(2):
            pltpu.make_async_copy(C.at[k, :, 2 * s + t, :], D.at[k, t, :, s, :], br.at[k]).start()

        def peer(r, _):
            d = (s + r) % SECS
            for t in range(2):
                remote(
                    C.at[k, :, 2 * d + t, :], D.at[k, t, :, s, :], bs.at[k], br.at[k], (c, d)
                ).start()
            return 0

        lax.fori_loop(1, SECS, peer, 0)

        return 0

    def both_of(i, _):
        level(i, 0)
        return give(i, 0)

    lax.fori_loop(0, LEV - 1, both_of, 0)
    level(LEV - 1, 0)

    total = jnp.zeros((LON, LAT), F32)
    for k in range(LEV):
        total += WATER_ABSORB + PIGMENT_ABSORB * saturating(pig[k])
    totals[s] = total

    def tell(r, _):
        remote(totals.at[s], totals.at[s], ts, tr_, (c, (s + r) % SECS)).start()
        return 0

    lax.fori_loop(1, SECS, tell, 0)
    give(LEV - 1, 0)
    sent = R.at[1, pl.ds(1, LON - 1)]

    def receive(i, _):
        k = lax.select(i == LEV - 1, LEV - 1, lax.select(i == LEV - 2, 0, i + 1))
        pltpu.make_async_copy(D.at[k], D.at[k], br.at[k]).wait()

        def unpack(n, _):
            t, half = n // 2, n % 2
            pieces = [
                D[k, t, v // 2, pl.ds(8 * half, 8), (v % 2) * HALF : (v % 2 + 1) * HALF]
                for v in range(2 * KEPT)
            ]
            pieces = unpacked(pieces)
            for group in range(2):
                for side in range(2):
                    lanes = slice(side * HALF, (side + 1) * HALF)
                    block = jnp.stack([pieces[2 * (8 * group + j) + side] for j in range(8)])
                    block = jnp.swapaxes(block, 0, 1)
                    here = wat_v[8 * group : 8 * group + 8, lanes] > 0
                    for d in range(8):
                        at = (t, LEV * (8 * half + d) + k, pl.ds(8 * group, 8), lanes)
                        sol_o[at] = jnp.where(here, block[d], sol_o[at])
            return 0

        lax.fori_loop(0, 4, unpack, 0)
        return 0

    original.wait()
    lax.fori_loop(0, LEV - 1, receive, 0)

    others = totals.at[pl.ds(0, SECS - 1)]
    pltpu.make_async_copy(others, others, tr_).wait()
    depth = jnp.zeros((LON, LAT), F32)
    for d in range(SECS):
        depth += totals[d] * jnp.where(d < s, 1.0, 0.0)
    light = CHLOROPHYLL_WARM * jnp.broadcast_to(lat_v[1:2, :], (LON, LAT)) * wet
    before = jnp.exp(-depth)
    for k in range(LEV):
        depth = depth + (WATER_ABSORB + PIGMENT_ABSORB * saturating(pig[k]))
        after = jnp.exp(-depth)
        thn_v[k] = thn_v[k] + light * (before - after)
        before = after
    outs.append(pltpu.make_async_copy(thn_v, th_o, osem.at[2]))
    outs[-1].start()

    receive(LEV - 1, 0)
    packed = goes.at[pl.ds(0, 2 * (SECS - 1) * KEPT * LAT // (8 * HALF))]

    def finish(k, _):
        pltpu.make_async_copy(sent, sent, fs.at[k]).wait()
        pltpu.make_async_copy(packed, packed, bs.at[k]).wait()
        return 0

    pltpu.make_async_copy(edge, edge, hs).wait()

    @pl.when(s > 0)
    def _():
        verticals[0].wait_send()

    @pl.when(s < SECS - 1)
    def _():
        verticals[1].wait_send()

    pltpu.make_async_copy(others, others, ts).wait()
    lax.fori_loop(0, LEV, finish, 0)
    for copy in outs:
        copy.wait()


def settle(*refs):
    given, made, sem = refs[:4], refs[4:8], refs[8]
    copies = [pltpu.make_async_copy(a, b, sem.at[i]) for i, (a, b) in enumerate(zip(given, made))]
    for copy in copies:
        copy.start()
    for copy in copies:
        copy.wait()


def on_device(thermal, flow, spreading, solute, lin, pre, ab, water):
    index = (np.arange(LAT, dtype=np.float64) + 0.5) * np.pi / LAT - np.pi / 2
    table = np.zeros((8, LAT), np.float32)
    table[0] = CORIOLIS * np.sin(index)
    table[1] = np.cos(index)
    hbm = pl.BlockSpec(memory_space=pltpu.HBM)
    dma = pltpu.SemaphoreType.DMA
    shapes = tuple(
        jax.ShapeDtypeStruct(a.shape, F32) for a in (thermal, flow, spreading, solute)
    )
    vmem = pl.BlockSpec(memory_space=pltpu.VMEM)
    given = (solute, flow, spreading, thermal, lin, pre, ab.reshape(1, TR), water, jnp.asarray(table))
    results = pl.pallas_call(
        kernel,
        out_shape=shapes,
        in_specs=[hbm] * 9,
        out_specs=(vmem,) * 4,
        scratch_shapes=[
            pltpu.VMEM((LEV + 2, LON + 2, TR, LAT), F32),
            pltpu.VMEM((LON, TR, LAT), F32),
            pltpu.VMEM((LEV, KEPT, TR, LAT), F32),
            pltpu.VMEM((LEV, 2, KEPT, SECS, LAT), F32),
            pltpu.VMEM((BITS * PIECES, 8, HALF), jnp.int32),
            pltpu.VMEM((BITS * PIECES, 8, HALF), jnp.int32),
            pltpu.VMEM((PIECES, 8, HALF), jnp.int32),
            pltpu.VMEM((PIECES, 8, HALF), jnp.int32),
            pltpu.VMEM((LEV, 7, LON, LAT), F32),
            pltpu.VMEM((2 * TR, LAT), BF16),
            pltpu.VMEM((2, LEV, LON, LAT), F32),
            pltpu.VMEM((LEV, LON, LAT), F32),
            pltpu.VMEM((LEV, LON, LAT), F32),
            pltpu.VMEM((TR, TR), F32),
            pltpu.VMEM((TR, TR), F32),
            pltpu.VMEM((1, TR), F32),
            pltpu.VMEM((LON, LAT), jnp.int32),
            pltpu.VMEM((8, LAT), F32),
            pltpu.VMEM((2, LON, LAT), F32),
            pltpu.VMEM((2, LON, LAT), F32),
            pltpu.VMEM((LON, LAT), F32),
            pltpu.VMEM((2, LEV, 8, LAT), F32),
            pltpu.VMEM((2, LEV, LON, LAT), F32),
            pltpu.VMEM((LEV, LON, LAT), F32),
            pltpu.VMEM((LEV, LON, LAT), F32),
            pltpu.VMEM((SECS, LON, LAT), F32),
            pltpu.VMEM((LEV, LON, LAT), F32),
            pltpu.VMEM((4, LON, LAT), jnp.int32),
            dma((8,)), dma((3,)), dma((5,)), dma((5,)),
            dma, dma((LEV,)), dma((LEV,)), dma((LEV,)), dma((2,)), dma((2,)), dma((LEV,)), dma((LEV,)),
            dma, dma, dma,
            pltpu.VMEM((2, KEPT, TR, LAT), F32),
            pltpu.VMEM((2, KEPT, TR, LAT), F32),
        ],
        compiler_params=pltpu.CompilerParams(
            collective_id=0, has_side_effects=True, vmem_limit_bytes=48 << 20
        ),
        name="ocean_step",
    )(*(pltpu.with_memory_space_constraint(a, pltpu.HBM) for a in given))
    return pl.pallas_call(
        settle,
        out_shape=shapes,
        in_specs=[vmem] * 4,
        out_specs=(hbm,) * 4,
        scratch_shapes=[dma((4,))],
        compiler_params=pltpu.CompilerParams(vmem_limit_bytes=16 << 20),
        name="settle",
    )(*results)


def solution(mesh):
    placed = (
        P("sec", "col", None),
        P(None, "sec", "col", None),
        P("sec", "col", None),
        P("sec", None, "col", None),
        P(),
        P(),
        P(),
        P("col", None),
    )
    return jax.shard_map(
        on_device,
        mesh=mesh,
        in_specs=placed,
        out_specs=placed[:1] + placed[1:4],
        check_vma=False,
    )
```
